256 devices in a mesh: src: 16 (over z, y_hi), tgt: 16 (over x, y_lo, core).
Axes of the slice: x: 4, y: 4 (y_hi: 2, y_lo: 2; y = y_hi * 2 + y_lo), z: 8, core: 2. Of those that a mesh axis runs over, the one named last changes fastest.
Arguments:
- frame_one: bfloat16 [256, 256, 128], P(('src', 'tgt')), may hold values from -36 to 36
- frame_two: bfloat16 [256, 256, 128], P(('src', 'tgt')), may hold values from -36 to 36
- conv_weight: bfloat16 [9, 128, 128], replicated, may hold values from -0.1875 to 0.1875
- proj_weight: bfloat16 [128, 128], replicated, may hold values from -0.5 to 0.5
Outputs:
- flow_forward: float32 [2, 256, 256], P(None, ('src', 'tgt'))
- flow_backward: float32 [2, 256, 256], P(None, ('src', 'tgt'))
The draws below stay inside these ranges and needn't reach their ends.
All inputs are finite; a program needn't handle non-finite values.
Results may differ from the reference program's by a relative error of at most 0.012.
The reference program's roundings to bfloat16 on the way (of `hidden` and `features`) count: a program that leaves them out, or rounds other values in their place, can miss the bound.
Values may be sent and summed in bfloat16 or wider, within the bound.
A program may use at most 64 MiB of HBM per device.

```python
import math
import jax
import jax.numpy as jnp
from jax import lax

C = 128
W = 256
H = 256


max_shift = 8


def frame_pair(key):
    padded_width = W + 2 * max_shift + 2
    base = jnp.clip(jax.random.normal(jax.random.fold_in(key, 11), (H, padded_width, C), jnp.float32), -6.0, 6.0)
    shifts = jax.random.randint(jax.random.fold_in(key, 12), (H,), -max_shift, max_shift + 1)
    fraction = jax.random.uniform(jax.random.fold_in(key, 13), (H,), jnp.float32, 0.2, 0.8)
    noise = jnp.clip(jax.random.normal(jax.random.fold_in(key, 14), (H, W, C), jnp.float32), -6.0, 6.0)
    magnitude = jax.random.randint(jax.random.fold_in(key, 16), (H,), 1, 5)
    direction = jax.random.randint(jax.random.fold_in(key, 17), (H,), 0, 2) * 2 - 1
    offset = (magnitude * direction).astype(jnp.int32)
    row_numbers = jnp.arange(H, dtype=jnp.int32)
    raised = row_numbers + offset
    inside = jnp.logical_and(raised >= 0, raised < H)
    anchor_rows = jnp.where(inside, raised, row_numbers - offset).astype(jnp.int32)
    source = base[:, max_shift + 1:max_shift + 1 + W, :]

    def displaced(image_row, shift_value, weight):
        nearer = lax.dynamic_slice_in_dim(image_row, max_shift + 1 + shift_value, W, 0)
        farther = lax.dynamic_slice_in_dim(image_row, max_shift + 2 + shift_value, W, 0)
        return (1.0 - weight) * nearer + weight * farther
    target = jax.vmap(displaced)(base[anchor_rows], shifts, fraction) + 0.3 * noise
    return (source, target)


def draw_frame_one(key, part):
    return frame_pair(key)[0].astype(jnp.bfloat16)


def draw_frame_two(key, part):
    return frame_pair(key)[1].astype(jnp.bfloat16)


def bell_draw(own_key, shape, spread, bound, kind=jnp.bfloat16):
    return jnp.clip(spread * jax.random.normal(own_key, shape, jnp.float32), -bound, bound).astype(kind)


def setup_inputs(seed: int = 0) -> dict:
    arg_keys = jax.random.split(jax.random.key(seed), 5)
    frame_one = draw_frame_one(jax.random.fold_in(arg_keys[4], 71), 0)
    frame_two = draw_frame_two(jax.random.fold_in(arg_keys[4], 71), 0)
    conv_weight = bell_draw(arg_keys[2], (9, C, C), (9 * C) ** -0.5, 0.1875)
    proj_weight = bell_draw(arg_keys[3], (C, C), C ** -0.5, 0.5)
    return dict(frame_one=frame_one, frame_two=frame_two, conv_weight=conv_weight, proj_weight=proj_weight)


def encode(stacked, conv_weight, proj_weight):
    height, columns = (stacked.shape[1], stacked.shape[2])
    padded = jnp.pad(stacked, ((0, 0), (1, 1), (1, 1), (0, 0)))
    total = jnp.zeros(stacked.shape, jnp.float32)
    for offset_row in range(3):
        for offset_col in range(3):
            window = padded[:, offset_row:offset_row + height, offset_col:offset_col + columns, :]
            total = total + jnp.dot(window, conv_weight[3 * offset_row + offset_col], preferred_element_type=jnp.float32)
    hidden = jax.nn.relu(total).astype(jnp.bfloat16)
    mixed = stacked.astype(jnp.float32) + jnp.dot(hidden, proj_weight, preferred_element_type=jnp.float32)
    return mixed.astype(jnp.bfloat16)

def merge_pair(former, latter):
    highest = jnp.maximum(former[0], latter[0])
    keep_former = jnp.exp(former[0] - highest)
    keep_latter = jnp.exp(latter[0] - highest)
    return (highest, former[1] * keep_former + latter[1] * keep_latter, former[2] * keep_former + latter[2] * keep_latter, former[3] * keep_former + latter[3] * keep_latter)

def reference(frame_one, frame_two, conv_weight, proj_weight):
    features = encode(jnp.stack([frame_one, frame_two]), conv_weight, proj_weight)
    factor = 1.0 / math.sqrt(C)
    source_flat = features[0].reshape(-1, C).astype(jnp.float32)
    target_flat = features[1].reshape(-1, C).astype(jnp.float32)
    coord_x = jnp.tile(jnp.arange(W, dtype=jnp.float32), H)
    coord_y = jnp.repeat(jnp.arange(H, dtype=jnp.float32), W)
    block_rows = math.gcd(H, max(1, 512 // W))
    blocks = H // block_rows
    block_size = block_rows * W

    def block_step(running, block_item):
        source_block, block_x, block_y = block_item
        scores = lax.dot_general(source_block, target_flat, (((1,), (1,)), ((), ())), precision=lax.Precision.HIGHEST, preferred_element_type=jnp.float32) * factor
        row_top = lax.optimization_barrier(jnp.max(scores, axis=1))
        row_weights = jnp.exp(scores - row_top[:, None])
        row_stats = (lax.optimization_barrier(jnp.sum(row_weights, axis=1)), lax.optimization_barrier(jnp.sum(row_weights * coord_x[None, :], axis=1)), lax.optimization_barrier(jnp.sum(row_weights * coord_y[None, :], axis=1)))
        column_top = lax.optimization_barrier(jnp.max(scores, axis=0))
        column_weights = jnp.exp(scores - column_top[None, :])
        column_stats = (column_top, lax.optimization_barrier(jnp.sum(column_weights, axis=0)), lax.optimization_barrier(jnp.sum(column_weights * block_x[:, None], axis=0)), lax.optimization_barrier(jnp.sum(column_weights * block_y[:, None], axis=0)))
        return (merge_pair(running, column_stats), row_stats)
    pixels = H * W
    empty_stats = (jnp.full((pixels,), -jnp.inf, jnp.float32), jnp.zeros((pixels,), jnp.float32), jnp.zeros((pixels,), jnp.float32), jnp.zeros((pixels,), jnp.float32))
    column_acc, row_parts = lax.scan(block_step, empty_stats, (source_flat.reshape(blocks, block_size, C), coord_x.reshape(blocks, block_size), coord_y.reshape(blocks, block_size)))
    row_total = row_parts[0].reshape(-1)
    flow_forward = jnp.stack([row_parts[1].reshape(-1) / row_total - coord_x, row_parts[2].reshape(-1) / row_total - coord_y]).reshape(2, H, W)
    flow_backward = jnp.stack([column_acc[2] / column_acc[1] - coord_x, column_acc[3] / column_acc[1] - coord_y]).reshape(2, H, W)
    return (flow_forward, flow_backward)
```

```python
import math

import jax
import jax.numpy as jnp
from jax import lax
from jax.experimental import pallas as pl
from jax.experimental.pallas import tpu as pltpu
from jax.sharding import PartitionSpec as P

F32 = jnp.float32
BF16 = jnp.bfloat16
MESH = pl.DeviceIdType.MESH
LOG2_SCALE = math.log2(math.e) / math.sqrt(128.0)
NORM_LIMIT = (96.0 / LOG2_SCALE) ** 2
WC = 16
CHUNKS = 256 // WC


def fused_kernel(
    f1_ref, f2_ref, cw_ref, pw_ref,
    ff_ref, fb_ref, flag_ref,
    halo, S, T, HL, R, Y, U, G, CC, rout, cout, rin, cin,
    halo_send, halo_recv, s_send, s_recv, t_send, t_recv, r_send, r_recv, c_send, c_recv,
):
    src = lax.axis_index("src")
    tgt = lax.axis_index("tgt")
    z = src // 2
    yh = lax.rem(src, 2)
    x = tgt // 4
    yl = lax.rem(tgt // 2, 2)
    c = lax.rem(tgt, 2)
    me = src * 16 + tgt
    k_own = yh * 8 + x * 2 + yl
    t_own = z * 2 + c

    def plane_peer(d):
        k = lax.rem(k_own + d, 16)
        return k, (z * 2 + k // 8, lax.rem(k // 2, 4) * 4 + lax.rem(k, 2) * 2 + c)

    def line_peer(d):
        t = lax.rem(t_own + d, 16)
        return t, ((t // 2) * 2 + yh, x * 4 + yl * 2 + lax.rem(t, 2))

    up = lax.rem(me + 255, 256)
    down = lax.rem(me + 1, 256)
    up_id = (up // 16, lax.rem(up, 16))
    down_id = (down // 16, lax.rem(down, 16))

    barrier = pltpu.get_barrier_semaphore()
    peers = [up_id, down_id]
    for d in range(1, 16):
        peers.append(plane_peer(d)[1])
        peers.append(line_peer(d)[1])
    for peer in peers:
        pl.semaphore_signal(barrier, inc=1, device_id=peer, device_id_type=MESH)
    pl.semaphore_wait(barrier, len(peers))

    def remote(source, target, send, recv, peer):
        return pltpu.make_async_remote_copy(
            src_ref=source, dst_ref=target, send_sem=send, recv_sem=recv,
            device_id=peer, device_id_type=MESH,
        )

    halos = []
    for frame, ref in ((0, f1_ref), (1, f2_ref)):
        halos.append(remote(ref.at[0], halo.at[0, frame], halo_send.at[0, frame], halo_recv.at[0, frame], down_id))
        halos.append(remote(ref.at[0], halo.at[1, frame], halo_send.at[1, frame], halo_recv.at[1, frame], up_id))
    for copy in halos:
        copy.start()
    zero_rows = jnp.zeros((256, 128), F32)

    def clear(k, carry):
        R[k] = zero_rows
        Y[k] = zero_rows
        U[k] = zero_rows
        G[k] = zero_rows
        return carry

    lax.fori_loop(0, 16, clear, 0)
    for copy in halos:
        copy.wait()

    def encode_rows(*accs):
        column = lax.broadcasted_iota(jnp.int32, (256, 128), 0)
        zero_bf = jnp.zeros((256, 128), BF16)
        zero_tap = jnp.zeros((128, 128), BF16)

        def side(left, right):
            return jnp.concatenate([left, right], axis=1)

        def tap_tile(half, m):
            rows = []
            for a in (0, 1) if half == 0 else (2, 3):
                tap = [
                    cw_ref[3 * a + b] if a < 3 and b < 3 else zero_tap
                    for b in ((0, 1) if m == 0 else (2, 3))
                ]
                rows.append(side(*tap))
            return jnp.concatenate(rows, axis=0)

        own = [f1_ref[0], f2_ref[0]]
        for half in range(2):
            for m in range(2):
                pltpu.matmul_push_rhs(tap_tile(half, m), 0, m)
            for frame in range(2):
                if half == 0:
                    lhs = side(jnp.where(me > 0, halo[0, frame], zero_bf), own[frame])
                else:
                    lhs = side(jnp.where(me < 255, halo[1, frame], zero_bf), zero_bf)
                for m in range(2):
                    pltpu.matmul_acc_lhs(accs[2 * m + frame], lhs, load_staged_rhs=0 if frame == 0 else None)
        pw = pw_ref[...]
        pltpu.matmul_push_rhs(jnp.concatenate([side(pw, zero_tap), side(zero_tap, pw)], axis=0), 0, 0)
        hidden = []
        for frame in range(2):
            first = pltpu.matmul_pop(accs[frame])
            third = pltpu.matmul_pop(accs[2 + frame])
            left = jnp.where(column == 0, 0.0, pltpu.roll(first[:, 0:128], 1, 0))
            right = jnp.where(column == 255, 0.0, pltpu.roll(third[:, 0:128], 255, 0))
            hidden.append(jnp.maximum(left + first[:, 128:256] + right, 0.0).astype(BF16))
        pltpu.matmul_acc_lhs(accs[0], side(*hidden), load_staged_rhs=0)
        mixed = pltpu.matmul_pop(accs[0])
        for frame in range(2):
            feature = (own[frame].astype(F32) + mixed[:, 128 * frame : 128 * frame + 128]).astype(BF16)
            wide = feature.astype(F32)
            norm = jnp.max(jnp.sum(wide * wide, axis=1, keepdims=True), axis=0, keepdims=True)
            norm_rows = jnp.broadcast_to(norm * 1.01, (16, 128)).astype(BF16)
            if frame == 0:
                S[k_own, 0:256, :] = feature
                S[k_own, 256:272, :] = norm_rows
            else:
                T[t_own, 0:256, :] = feature
                T[t_own, 256:272, :] = norm_rows

    pl.run_scoped(encode_rows, *[pltpu.ACC(m)((256, 256), F32) for m in (0, 0, 1, 1)])

    s_copies = []
    t_copies = []
    for d in range(1, 16):
        _, peer = plane_peer(d)
        s_copies.append(remote(S.at[k_own], S.at[k_own], s_send.at[d], s_recv.at[k_own], peer))
        _, peer = line_peer(d)
        t_copies.append(remote(T.at[t_own], T.at[t_own], t_send.at[d], t_recv.at[t_own], peer))
    for s_copy, t_copy in zip(s_copies, t_copies):
        s_copy.start()
        t_copy.start()
    for d in range(1, 16):
        k, peer = plane_peer(d)
        remote(S.at[k], S.at[k], s_send.at[d], s_recv.at[k], peer).wait_recv()
        t, peer = line_peer(d)
        remote(T.at[t], T.at[t], t_send.at[d], t_recv.at[t], peer).wait_recv()

    def split(k, carry):
        value = S[k, 0:256, :].astype(F32) * LOG2_SCALE
        head = value.astype(BF16)
        HL[k, :, 0:128] = head
        HL[k, :, 128:256] = (value - head.astype(F32)).astype(BF16)
        return carry

    lax.fori_loop(0, 16, split, 0)
    base_rows = (yh * 16 + x * 4 + yl * 2).astype(F32)
    base_cols = (z * 32 + c).astype(F32)

    def tile(*accs):
        slots = ((accs[0:16], accs[16:32]), (accs[32:48], accs[48:64]))

        def push(zt):
            for m in range(2):
                w = T[2 * zt + m, 0:256, :]
                pltpu.matmul_push_rhs(jnp.concatenate([w, w], axis=1), 0, m, transpose=True)

        def issue(slot, chunk, load):
            for k in range(15, -1, -1):
                lhs = HL[k, pl.ds(chunk * WC, WC), :]
                for m in range(2):
                    pltpu.matmul_acc_lhs(
                        slots[slot][m][k], lhs, load_staged_rhs=0 if load and k == 15 else None
                    )

        def process(slot, chunk):
            window = pl.ds(chunk * WC, WC)
            total = [None, None]
            ranked = [None, None]
            for k in range(15, -1, -1):
                e = [jnp.exp2(pltpu.matmul_pop(slots[slot][m][k])) for m in range(2)]
                odd = e[1][:, :128] + e[1][:, 128:]
                even = e[0][:, :128] + e[0][:, 128:]
                r = R[k, window, :] + (odd + even)
                R[k, window, :] = r
                Y[k, window, :] = Y[k, window, :] + r
                U[k, window, :] = U[k, window, :] + odd
                G[k, window, :] = G[k, window, :] + (e[1][:, 128:] + e[0][:, 128:])
                for m in range(2):
                    total[m] = e[m] if k == 15 else total[m] + e[m]
                    if k == 15:
                        ranked[m] = total[m]
                    elif k > 0:
                        ranked[m] = ranked[m] + total[m]
            weight = (lax.broadcasted_iota(jnp.int32, (WC, 256), 0) + chunk * WC).astype(F32)
            for m in range(2):
                CC[m, 0] += jnp.sum(total[m].reshape(WC // 8, 8, 256), axis=0)
                CC[m, 1] += jnp.sum((total[m] * weight).reshape(WC // 8, 8, 256), axis=0)
                CC[m, 2] += jnp.sum(ranked[m].reshape(WC // 8, 8, 256), axis=0)

        def per_pair(step, carry):
            zt = 7 - step
            CC[...] = jnp.zeros_like(CC)

            def inner(i, inner_carry):
                issue(1, 2 * i + 1, False)
                process(0, 2 * i)
                issue(0, 2 * i + 2, False)
                process(1, 2 * i + 1)
                return inner_carry

            lax.fori_loop(0, CHUNKS // 2 - 1, inner, 0)
            issue(1, CHUNKS - 1, False)
            process(0, CHUNKS - 2)
            push(lax.rem(zt + 7, 8))
            issue(0, 0, True)
            process(1, CHUNKS - 1)
            for m in range(2):
                count = jnp.sum(CC[m, 0], axis=0, keepdims=True)
                cout[2 * zt + m, 0:1, :] = count
                cout[2 * zt + m, 1:2, :] = jnp.sum(CC[m, 1], axis=0, keepdims=True)
                cout[2 * zt + m, 2:3, :] = (
                    2.0 * jnp.sum(CC[m, 2], axis=0, keepdims=True) + base_cols * count
                )
            return carry

        push(7)
        issue(0, 0, True)
        lax.fori_loop(0, 8, per_pair, 0)
        for k in range(16):
            for m in range(2):
                CC[m, 0] = pltpu.matmul_pop(slots[0][m][k])[:8]

    pl.run_scoped(
        tile, *[pltpu.ACC(m)((WC, 256), F32) for m in (0, 1, 0, 1) for _ in range(16)]
    )

    s_norm = jnp.broadcast_to(
        jnp.max(jnp.max(S[:, 256:272, :].astype(F32), axis=0)[0:8], axis=(0, 1), keepdims=True), (1, 256)
    )
    t_norm = jnp.broadcast_to(
        jnp.max(jnp.max(T[:, 256:272, :].astype(F32), axis=0)[0:8], axis=(0, 1), keepdims=True), (1, 256)
    )

    lane = lax.broadcasted_iota(jnp.int32, (128, 128), 0).astype(F32)

    def finish(k, carry):
        for h in range(2):
            w = slice(h * 128, h * 128 + 128)
            r = R[k, w, :].T
            g = G[k, w, :].T
            y = (32.0 * (Y[k, w, :] - R[k, w, :]) + U[k, w, :]).T
            count = jnp.sum(r, axis=0, keepdims=True)
            rout[k, 0:1, w] = count
            rout[k, 1:2, w] = jnp.sum(r * lane + 128.0 * g, axis=0, keepdims=True)
            rout[k, 2:3, w] = jnp.sum(y, axis=0, keepdims=True) + base_rows * count
        rout[k, 3:4, :] = t_norm
        cout[k, 3:4, :] = s_norm
        return carry

    lax.fori_loop(0, 16, finish, 0)

    out_copies = []
    for d in range(1, 16):
        k, peer = plane_peer(d)
        out_copies.append(remote(rout.at[k], rin.at[k_own], r_send.at[d], r_recv.at[k_own], peer))
        t, peer = line_peer(d)
        out_copies.append(remote(cout.at[t], cin.at[t_own], c_send.at[d], c_recv.at[t_own], peer))
    for copy in out_copies:
        copy.start()
    rin[k_own] = rout[k_own]
    cin[t_own] = cout[t_own]
    for d in range(1, 16):
        k, peer = plane_peer(d)
        remote(rout.at[k], rin.at[k], r_send.at[d], r_recv.at[k], peer).wait_recv()
        t, peer = line_peer(d)
        remote(cout.at[t], cin.at[t], c_send.at[d], c_recv.at[t], peer).wait_recv()

    coord_x = lax.broadcasted_iota(jnp.int32, (1, 256), 1).astype(F32)
    coord_y = me.astype(F32)
    bound = []
    for blocks, out in ((rin, ff_ref), (cin, fb_ref)):
        merged = jnp.sum(blocks[...], axis=0)
        out[0, 0:1, :] = merged[1:2] / merged[0:1] - coord_x
        out[1, 0:1, :] = merged[2:3] / merged[0:1] - coord_y
        bound.append(jnp.max(blocks[...], axis=0)[3:4, 0:128])
    flag_ref[...] = jnp.broadcast_to(
        jnp.where(bound[0] * bound[1] <= NORM_LIMIT, 1.0, 0.0), (8, 128)
    )

    for copy in s_copies + t_copies + out_copies:
        copy.wait_send()


def fused(frame_one, frame_two, conv_weight, proj_weight):
    vmem = pl.BlockSpec(memory_space=pltpu.VMEM)
    dma = pltpu.SemaphoreType.DMA
    return pl.pallas_call(
        fused_kernel,
        out_shape=[
            jax.ShapeDtypeStruct((2, 1, 256), F32),
            jax.ShapeDtypeStruct((2, 1, 256), F32),
            jax.ShapeDtypeStruct((8, 128), F32),
        ],
        in_specs=[vmem] * 4,
        out_specs=[vmem] * 3,
        scratch_shapes=[
            pltpu.VMEM((2, 2, 256, 128), BF16),
            pltpu.VMEM((16, 272, 128), BF16),
            pltpu.VMEM((16, 272, 128), BF16),
            pltpu.VMEM((16, 256, 256), BF16),
            pltpu.VMEM((16, 256, 128), F32),
            pltpu.VMEM((16, 256, 128), F32),
            pltpu.VMEM((16, 256, 128), F32),
            pltpu.VMEM((16, 256, 128), F32),
            pltpu.VMEM((2, 3, 8, 256), F32),
            pltpu.VMEM((16, 8, 256), F32),
            pltpu.VMEM((16, 8, 256), F32),
            pltpu.VMEM((16, 8, 256), F32),
            pltpu.VMEM((16, 8, 256), F32),
            dma((2, 2)), dma((2, 2)),
            dma((16,)), dma((16,)), dma((16,)), dma((16,)),
            dma((16,)), dma((16,)), dma((16,)), dma((16,)),
        ],
        compiler_params=pltpu.CompilerParams(
            collective_id=0,
            has_side_effects=True,
            vmem_limit_bytes=48 << 20,
        ),
        name="flow",
    )(frame_one, frame_two, conv_weight, proj_weight)


def padded_2(block, sides, width):
    for axis, dim in sides:
        count = lax.axis_size(axis)
        forward = [(i, i + 1) for i in range(count - 1)]
        backward = [(target, source) for source, target in forward]
        low = lax.ppermute(
            lax.slice_in_dim(block, block.shape[dim] - width, None, axis=dim), axis, forward
        )
        high = lax.ppermute(lax.slice_in_dim(block, 0, width, axis=dim), axis, backward)
        block = jnp.concatenate([low, block, high], axis=dim)
    return block


def merged(value, axis, join):
    pieces = jax.tree.map(lambda part: lax.all_gather(part, axis), value)
    head = jax.tree.map(lambda part: part[0], pieces)
    tail = jax.tree.map(lambda part: part[1:], pieces)
    subtotal, _ = lax.scan(lambda subtotal, piece: (join(subtotal, piece), None), head, tail)
    return subtotal


def encode(stacked, conv_weight, proj_weight):
    padded = padded_2(stacked, ((("src", "tgt"), 1),), 1)
    padded = jnp.pad(padded, ((0, 0), (0, 0), (1, 1), (0, 0)))
    strip_rows, columns = (stacked.shape[1], stacked.shape[2])
    total = jnp.zeros(stacked.shape, jnp.float32)
    for offset_row in range(3):
        for offset_col in range(3):
            window = padded[
                :, offset_row : offset_row + strip_rows, offset_col : offset_col + columns, :
            ]
            total = total + jnp.dot(
                window, conv_weight[3 * offset_row + offset_col], preferred_element_type=jnp.float32
            )
    hidden = jax.nn.relu(total).astype(jnp.bfloat16)
    mixed = stacked.astype(jnp.float32) + jnp.dot(
        hidden, proj_weight, preferred_element_type=jnp.float32
    )
    return mixed.astype(jnp.bfloat16)


def merge_pair(former, latter):
    highest = jnp.maximum(former[0], latter[0])
    keep_former = jnp.exp(former[0] - highest)
    keep_latter = jnp.exp(latter[0] - highest)
    return (
        highest,
        former[1] * keep_former + latter[1] * keep_latter,
        former[2] * keep_former + latter[2] * keep_latter,
        former[3] * keep_former + latter[3] * keep_latter,
    )


def tile_stats(piece_block, block_x, block_y, fixed_flat, fixed_x, fixed_y, factor):
    scores = (
        lax.dot_general(
            piece_block, fixed_flat, (((1,), (1,)), ((), ())), preferred_element_type=jnp.float32
        )
        * factor
    )
    row_top = jnp.max(scores, axis=1)
    row_weights = jnp.exp(scores - row_top[:, None])
    row_stats = (
        row_top,
        jnp.sum(row_weights, axis=1),
        jnp.sum(row_weights * fixed_x[None, :], axis=1),
        jnp.sum(row_weights * fixed_y[None, :], axis=1),
    )
    column_top = jnp.max(scores, axis=0)
    column_weights = jnp.exp(scores - column_top[None, :])
    column_stats = (
        column_top,
        jnp.sum(column_weights, axis=0),
        jnp.sum(column_weights * block_x[:, None], axis=0),
        jnp.sum(column_weights * block_y[:, None], axis=0),
    )
    return (row_stats, column_stats)


def general(frame_one, frame_two, conv_weight, proj_weight):
    features = encode(jnp.stack([frame_one, frame_two]), conv_weight, proj_weight)
    source_feat = features[0]
    target_feat = features[1]
    strip_rows, columns, channels = frame_one.shape
    src_index = lax.axis_index("src")
    tgt_index = lax.axis_index("tgt")
    src_count = lax.axis_size("src")
    tgt_count = lax.axis_size("tgt")
    factor = 1.0 / math.sqrt(channels)
    source_pixels = strip_rows * tgt_count * columns
    target_pixels = strip_rows * src_count * columns
    own_pixels = strip_rows * columns

    def pixel_coords(row_numbers):
        coord_y = jnp.repeat(row_numbers.astype(jnp.float32), columns)
        coord_x = jnp.tile(jnp.arange(columns, dtype=jnp.float32), row_numbers.shape[0])
        return (coord_x, coord_y)

    def empty_stats(count):
        zeros_line = jnp.zeros((count,), jnp.float32)
        return (jnp.full((count,), -jnp.inf, jnp.float32), zeros_line, zeros_line, zeros_line)

    target_tile = lax.all_gather(target_feat, "src", axis=0, tiled=True)
    whole_row = jnp.arange(strip_rows * src_count, dtype=jnp.int32)
    tile_x, tile_y = pixel_coords(
        (whole_row // strip_rows * tgt_count + tgt_index) * strip_rows + whole_row % strip_rows
    )
    fixed_flat = target_tile.reshape(-1, channels)
    shard_piece = lax.all_gather(source_feat, "tgt", axis=0, tiled=True)
    piece_rows = shard_piece.shape[0]
    block_rows = math.gcd(piece_rows, max(1, 512 // columns))
    blocks = piece_rows // block_rows
    block_size = block_rows * columns
    piece_x, piece_y = pixel_coords(
        src_index * tgt_count * strip_rows + jnp.arange(piece_rows, dtype=jnp.int32)
    )

    def block_step(fixed_acc, block_item):
        piece_block, block_x, block_y = block_item
        row_stats, column_stats = tile_stats(
            piece_block, block_x, block_y, fixed_flat, tile_x, tile_y, factor
        )
        return (merge_pair(fixed_acc, column_stats), row_stats)

    fixed_acc, row_parts = lax.scan(
        block_step,
        (empty_stats(target_pixels), empty_stats(source_pixels))[0],
        (
            shard_piece.reshape(blocks, block_size, channels),
            piece_x.reshape(blocks, block_size),
            piece_y.reshape(blocks, block_size),
        ),
    )
    placed = tuple((segment.reshape(-1) for segment in row_parts))
    fixed_acc, piece_acc = (fixed_acc, placed)
    source_stats, target_stats = (piece_acc, fixed_acc)
    own_x, own_y = pixel_coords(
        (src_index * tgt_count + tgt_index) * strip_rows + jnp.arange(strip_rows, dtype=jnp.int32)
    )
    merged_rows = merged(source_stats, "tgt", merge_pair)
    merged_cols = merged(target_stats, "src", merge_pair)
    source_sums = [
        lax.dynamic_slice_in_dim(member, tgt_index * own_pixels, own_pixels, 0)
        for member in merged_rows[1:]
    ]
    target_sums = [
        lax.dynamic_slice_in_dim(member, src_index * own_pixels, own_pixels, 0)
        for member in merged_cols[1:]
    ]
    flow_forward = jnp.stack(
        [source_sums[1] / source_sums[0] - own_x, source_sums[2] / source_sums[0] - own_y]
    ).reshape(2, strip_rows, columns)
    flow_backward = jnp.stack(
        [target_sums[1] / target_sums[0] - own_x, target_sums[2] / target_sums[0] - own_y]
    ).reshape(2, strip_rows, columns)
    return (flow_forward, flow_backward)


def on_device(frame_one, frame_two, conv_weight, proj_weight):
    flow_forward, flow_backward, flag = fused(frame_one, frame_two, conv_weight, proj_weight)
    return lax.cond(
        flag[0, 0] > 0.5,
        lambda *_: (flow_forward, flow_backward),
        general,
        frame_one, frame_two, conv_weight, proj_weight,
    )


def solution(mesh):
    in_specs = (P(("src", "tgt"), None, None), P(("src", "tgt"), None, None), P(), P())
    out_specs = (P(None, ("src", "tgt"), None), P(None, ("src", "tgt"), None))
    return jax.shard_map(
        on_device, mesh=mesh, in_specs=in_specs, out_specs=out_specs, check_vma=False
    )
```

```python
import math

import jax
import jax.numpy as jnp
from jax import lax
from jax.experimental import pallas as pl
from jax.experimental.pallas import tpu as pltpu
from jax.sharding import PartitionSpec as P

F32 = jnp.float32
BF16 = jnp.bfloat16
FLAT = pl.DeviceIdType.LOGICAL
LOG2_SCALE = math.log2(math.e) / math.sqrt(128.0)
NORM_LIMIT = (96.0 / LOG2_SCALE) ** 2
WC = 16
CHUNKS = 256 // WC


def fused_kernel(
    f1_ref, f2_ref, cw_ref, pw_ref,
    ff_ref, fb_ref, flag_ref,
    halo, S, T, HL, R, Y, G, CC, rout, cout, rin, cin,
    halo_send, halo_recv, s_send, s_recv, t_send, t_pass, t_recv, r_send, r_recv, c_send, c_recv,
):
    src = lax.axis_index("src")
    tgt = lax.axis_index("tgt")
    z = lax.div(src, 2)
    x = lax.div(tgt, 4)
    c = lax.rem(tgt, 2)
    y = lax.rem(src, 2) * 2 + lax.rem(lax.div(tgt, 2), 2)
    me = src * 16 + tgt

    def x_slots(d):
        return 2 * lax.rem(x + d, 4)

    def y_slots(d):
        row = lax.rem(y + d, 4)
        return 8 * lax.div(row, 2) + lax.rem(row, 2)

    slots_x = [x_slots(d) for d in range(4)]
    slots_y = [y_slots(d) for d in range(4)]
    k_own = slots_x[0] + slots_y[0]
    t_own = z * 2 + c
    plane = z * 32 + c
    line = 2 * k_own
    partner = plane + line + 1 - 2 * c

    def line_z(step):
        return lax.rem(z + 8 + (2 * lax.rem(step, 2) - 1) * lax.div(step + 1, 2), 8)

    up = lax.rem(me + 255, 256)
    down = lax.rem(me + 1, 256)

    barrier = pltpu.get_barrier_semaphore()
    peers = [up, down, partner]
    for d in range(1, 8):
        for pc in range(2):
            peers.append(32 * lax.rem(z + d, 8) + line + pc)
    for d in range(1, 16):
        peers.append(plane + 2 * lax.rem(k_own + d, 16))
    for peer in peers:
        pl.semaphore_signal(barrier, inc=1, device_id=peer, device_id_type=FLAT)
    zero_rows = jnp.zeros((256, 128), F32)

    def clear(k, carry):
        R[k] = zero_rows
        Y[k] = zero_rows
        G[k] = zero_rows
        return carry

    lax.fori_loop(0, 16, clear, 0)
    pl.semaphore_wait(barrier, len(peers))

    def remote(source, target, send, recv, peer):
        return pltpu.make_async_remote_copy(
            src_ref=source, dst_ref=target, send_sem=send, recv_sem=recv,
            device_id=peer, device_id_type=FLAT,
        )

    halos = []
    for frame, ref in ((0, f1_ref), (1, f2_ref)):
        halos.append(remote(ref.at[0], halo.at[0, frame], halo_send.at[0, frame], halo_recv.at[0, frame], down))
        halos.append(remote(ref.at[0], halo.at[1, frame], halo_send.at[1, frame], halo_recv.at[1, frame], up))
    for copy in halos:
        copy.start()
    for copy in halos:
        copy.wait()

    def encode_rows(*accs):
        column = lax.broadcasted_iota(jnp.int32, (256, 128), 0)
        zero_bf = jnp.zeros((256, 128), BF16)
        zero_tap = jnp.zeros((128, 128), BF16)

        def side(left, right):
            return jnp.concatenate([left, right], axis=1)

        def tap_tile(half, m):
            rows = []
            for a in (0, 1) if half == 0 else (2, 3):
                tap = [
                    cw_ref[3 * a + b] if a < 3 and b < 3 else zero_tap
                    for b in ((0, 1) if m == 0 else (2, 3))
                ]
                rows.append(side(*tap))
            return jnp.concatenate(rows, axis=0)

        own = [f1_ref[0], f2_ref[0]]
        for half in range(2):
            for m in range(2):
                pltpu.matmul_push_rhs(tap_tile(half, m), 0, m)
            for frame in range(2):
                if half == 0:
                    lhs = side(jnp.where(me > 0, halo[0, frame], zero_bf), own[frame])
                else:
                    lhs = side(jnp.where(me < 255, halo[1, frame], zero_bf), zero_bf)
                for m in range(2):
                    pltpu.matmul_acc_lhs(accs[2 * m + frame], lhs, load_staged_rhs=0 if frame == 0 else None)
        pw = pw_ref[...]
        pltpu.matmul_push_rhs(jnp.concatenate([side(pw, zero_tap), side(zero_tap, pw)], axis=0), 0, 0)
        hidden = []
        for frame in range(2):
            first = pltpu.matmul_pop(accs[frame])
            third = pltpu.matmul_pop(accs[2 + frame])
            left = jnp.where(column == 0, 0.0, pltpu.roll(first[:, 0:128], 1, 0))
            right = jnp.where(column == 255, 0.0, pltpu.roll(third[:, 0:128], 255, 0))
            hidden.append(jnp.maximum(left + first[:, 128:256] + right, 0.0).astype(BF16))
        pltpu.matmul_acc_lhs(accs[0], side(*hidden), load_staged_rhs=0)
        mixed = pltpu.matmul_pop(accs[0])
        for frame in range(2):
            feature = (own[frame].astype(F32) + mixed[:, 128 * frame : 128 * frame + 128]).astype(BF16)
            wide = feature.astype(F32)
            norm = jnp.max(jnp.sum(wide * wide, axis=1, keepdims=True), axis=0, keepdims=True)
            norm_rows = jnp.broadcast_to(norm * 1.01, (16, 128)).astype(BF16)
            if frame == 0:
                S[k_own, 0:16, :] = norm_rows
                S[k_own, 16:272, :] = feature
            else:
                T[t_own, 0:16, :] = norm_rows
                T[t_own, 16:272, :] = feature

    pl.run_scoped(encode_rows, *[pltpu.ACC(m)((256, 256), F32) for m in (0, 0, 1, 1)])

    parts = (slice(0, 144), slice(144, 272))
    waiting = []
    sent = [0, 0]

    def send_half(half, k, to):
        ref = S.at[k, parts[half]]
        copy = remote(ref, ref, s_send.at[half, sent[half]], s_recv.at[half, k], plane + 2 * to)
        sent[half] += 1
        copy.start()
        waiting.append(copy)

    def split(half, k):
        w = slice(128 * half, 128 * half + 128)
        value = S[k, 16 + 128 * half : 144 + 128 * half, :].astype(F32) * LOG2_SCALE
        head = value.astype(BF16)
        HL[k, w, 0:128] = head
        HL[k, w, 128:256] = (value - head.astype(F32)).astype(BF16)

    def arrive(half, k):
        ref = S.at[k, parts[half]]
        remote(ref, ref, s_send.at[half, 0], s_recv.at[half, k], partner).wait_recv()

    first = (slots_x, slots_y)
    second = (slots_y, slots_x)
    odd_x = lax.rem(x, 2)
    odd_y = lax.rem(y, 2)

    def turned(half, d, flip):
        here = odd_x if half == 0 else odd_y
        odd = here if d % 2 == 0 else 1 - here
        if flip:
            odd = 1 - odd
        return second[half][1] + odd * (second[half][3] - second[half][1])

    for d in (1, 3, 2):
        for half in range(2):
            send_half(half, k_own, first[half][d] + second[half][0])
    own_ref = T.at[t_own]
    copy = remote(own_ref, own_ref, t_send.at[0], t_recv.at[t_own], partner)
    copy.start()
    waiting.append(copy)
    for step in range(1, 8):
        copy = remote(own_ref, own_ref, t_send.at[step], t_recv.at[t_own], 32 * line_z(step) + line + c)
        copy.start()
        waiting.append(copy)
    for d in (0, 1, 3, 2):
        for half in range(2):
            k = first[half][d] + second[half][0]
            if d:
                arrive(half, k)
            for e in (1, 3):
                send_half(half, k, first[half][0] + second[half][e])
        for half in range(2):
            split(half, first[half][d] + second[half][0])
    for d in (0, 1, 3, 2):
        for half in range(2):
            k = first[half][d] + turned(half, d, True)
            arrive(half, k)
            send_half(half, k, first[half][0] + turned(half, d, False))
        for half in range(2):
            split(half, first[half][d] + turned(half, d, True))
    for far in (False, True):
        for d in (0, 1, 3, 2):
            for half in range(2):
                k = first[half][d] + (second[half][2] if far else turned(half, d, False))
                arrive(half, k)
                split(half, k)

    def line_ref(step, pc):
        t = line_z(step) * 2 + pc
        return t, T.at[t]

    def pass_on(step):
        t, ref = line_ref(step, c)
        remote(ref, ref, t_send.at[0], t_recv.at[t], partner).wait_recv()
        remote(ref, ref, t_pass.at[step], t_recv.at[t], partner).start()

    def passed(step):
        t, ref = line_ref(step, 1 - c)
        remote(ref, ref, t_send.at[0], t_recv.at[t], partner).wait_recv()

    def largest(rows):
        return jnp.max(jnp.max(rows, axis=0)[0:8], axis=(0, 1), keepdims=True)

    s_norm = jnp.broadcast_to(largest(S[:, 0:16, :].astype(F32)), (1, 256))

    base_rows = line.astype(F32)
    base_cols = plane.astype(F32)

    def send_column(zt, m):
        t = 2 * zt + m

        @pl.when(t != t_own)
        def _():
            remote(
                cout.at[t], cin.at[t_own], c_send.at[t], c_recv.at[t_own], 32 * zt + line + m
            ).start()

        @pl.when(t == t_own)
        def _():
            cin[t] = cout[t]

    def tile(*accs):
        slots = ((accs[0:16], accs[16:32]), (accs[32:48], accs[48:64]))

        def push(zt):
            for m in range(2):
                w = T[2 * zt + m, 16:272, :]
                pltpu.matmul_push_rhs(jnp.concatenate([w, w], axis=1), 0, m, transpose=True)

        def issue(slot, chunk, load):
            for k in range(15, -1, -1):
                lhs = HL[k, pl.ds(chunk * WC, WC), :]
                for m in range(2):
                    pltpu.matmul_acc_lhs(
                        slots[slot][m][k], lhs, load_staged_rhs=0 if load and k == 15 else None
                    )

        def process(slot, chunk, row_weight):
            window = pl.ds(chunk * WC, WC)
            total = [None, None]
            ranked = [None, None]
            for k in range(15, -1, -1):
                e = [jnp.exp2(pltpu.matmul_pop(slots[slot][m][k])) for m in range(2)]
                odd = e[1][:, :128] + e[1][:, 128:]
                both = odd + (e[0][:, :128] + e[0][:, 128:])
                R[k, window, :] = R[k, window, :] + both
                Y[k, window, :] = Y[k, window, :] + (both * row_weight + odd)
                G[k, window, :] = G[k, window, :] + (e[1][:, 128:] + e[0][:, 128:])
                for m in range(2):
                    total[m] = e[m] if k == 15 else total[m] + e[m]
                    if k == 15:
                        ranked[m] = total[m]
                    elif k > 0:
                        ranked[m] = ranked[m] + total[m]
            weight = (lax.broadcasted_iota(jnp.int32, (WC, 256), 0) + chunk * WC).astype(F32)
            for m in range(2):
                CC[m, 0] += jnp.sum(total[m].reshape(WC // 8, 8, 256), axis=0)
                CC[m, 1] += jnp.sum((total[m] * weight).reshape(WC // 8, 8, 256), axis=0)
                CC[m, 2] += jnp.sum(ranked[m].reshape(WC // 8, 8, 256), axis=0)

        def per_pair(step, carry):
            zt = line_z(step)
            row_weight = (zt * 32).astype(F32)

            @pl.when(step > 0)
            def _():
                for m in range(2):
                    send_column(line_z(step - 1), m)

            @pl.when(step < 6)
            def _():
                pass_on(step + 2)

            CC[...] = jnp.zeros_like(CC)

            def inner(i, inner_carry):
                issue(1, 2 * i + 1, False)
                process(0, 2 * i, row_weight)
                issue(0, 2 * i + 2, False)
                process(1, 2 * i + 1, row_weight)
                return inner_carry

            lax.fori_loop(0, CHUNKS // 2 - 1, inner, 0)

            @pl.when(step < 7)
            def _():
                passed(step + 1)

            issue(1, CHUNKS - 1, False)
            process(0, CHUNKS - 2, row_weight)
            push(line_z(lax.rem(step + 1, 8)))
            issue(0, 0, True)
            process(1, CHUNKS - 1, row_weight)
            for m in range(2):
                count = jnp.sum(CC[m, 0], axis=0, keepdims=True)
                cout[2 * zt + m, 0:1, :] = count
                cout[2 * zt + m, 1:2, :] = jnp.sum(CC[m, 1], axis=0, keepdims=True)
                cout[2 * zt + m, 2:3, :] = (
                    2.0 * jnp.sum(CC[m, 2], axis=0, keepdims=True) + base_cols * count
                )
                cout[2 * zt + m, 3:4, :] = s_norm
            return carry

        passed(0)
        pass_on(1)
        push(line_z(0))
        issue(0, 0, True)
        lax.fori_loop(0, 8, per_pair, 0)
        for k in range(16):
            for m in range(2):
                CC[m, 0] = pltpu.matmul_pop(slots[0][m][k])[:8]

    pl.run_scoped(
        tile, *[pltpu.ACC(m)((WC, 256), F32) for m in (0, 1, 0, 1) for _ in range(16)]
    )

    lane = lax.broadcasted_iota(jnp.int32, (8, 128), 1)
    lane_weight = lane.astype(F32)
    t_norm = jnp.broadcast_to(largest(T[:, 0:16, :].astype(F32)), (8, 128))

    def fold(values):
        shift = 1
        while len(values) > 1:
            keep = (lane // shift) % 2 == 0
            values = [
                jnp.where(keep, values[i], values[i + 1])
                + pltpu.roll(jnp.where(keep, values[i + 1], values[i]), 128 - shift, 1)
                for i in range(0, len(values), 2)
            ]
            shift *= 2
        value = values[0]
        value = value + pltpu.roll(value, 64, 1)
        return value + pltpu.roll(value, 32, 1)

    for m in range(2):
        send_column(line_z(7), m)

    def finish(k):
        rows = [R[k, 8 * g : 8 * g + 8, :] for g in range(32)]
        count = fold(rows)
        col_x = fold([r * lane_weight + 128.0 * G[k, 8 * g : 8 * g + 8, :] for g, r in enumerate(rows)])
        col_y = fold([Y[k, 8 * g : 8 * g + 8, :] for g in range(32)]) + base_rows * count
        rout[k] = jnp.where(lane < 32, count, jnp.where(lane < 64, col_x, jnp.where(lane < 96, col_y, t_norm)))

    def send_row(d):
        k = lax.rem(k_own + d, 16)
        return remote(rout.at[k], rin.at[k_own], r_send.at[k], r_recv.at[k_own], plane + 2 * k)

    def two_rows(i, carry):
        for u in (1, 2):
            finish(lax.rem(k_own + 2 * i + u, 16))

        @pl.when(i > 0)
        def _():
            for u in (1, 2):
                send_row(2 * i - 2 + u).start()

        return carry

    lax.fori_loop(0, 8, two_rows, 0)
    send_row(15).start()
    rin[k_own] = rout[k_own]

    for d in range(1, 16):
        t = lax.rem(t_own + d, 16)
        remote(cout.at[t], cin.at[t], c_send.at[t], c_recv.at[t], partner).wait_recv()
    merged = jnp.sum(cin[...], axis=0)
    coord_x = lax.broadcasted_iota(jnp.int32, (1, 256), 1).astype(F32)
    coord_y = me.astype(F32)
    fb_ref[0, 0:1, :] = merged[1:2] / merged[0:1] - coord_x
    fb_ref[1, 0:1, :] = merged[2:3] / merged[0:1] - coord_y
    s_bound = jnp.max(jnp.max(cin[...], axis=0)[3:4, 0:128], axis=1, keepdims=True)
    for d in range(1, 16):
        k = lax.rem(k_own + d, 16)
        remote(rout.at[k], rin.at[k], r_send.at[k], r_recv.at[k], partner).wait_recv()
    sums = jnp.sum(rin[...], axis=0)
    sublane = lax.broadcasted_iota(jnp.int32, (8, 128), 0)
    flows = (
        pltpu.roll(sums, 96, 1) / sums - (lane * 8 + sublane).astype(F32),
        pltpu.roll(sums, 64, 1) / sums - coord_y,
    )
    for i, value in enumerate(flows):
        for h in range(2):
            spread = jnp.take_along_axis(value, 16 * h + lane // 8, axis=1)
            ff_ref[i, 0:1, 128 * h : 128 * h + 128] = jnp.sum(
                jnp.where(sublane == lane % 8, spread, 0.0), axis=0, keepdims=True
            )
    t_bound = jnp.max(
        jnp.where(lane >= 96, jnp.max(rin[...], axis=0), 0.0), axis=(0, 1), keepdims=True
    )
    flag_ref[...] = jnp.broadcast_to(
        jnp.where(s_bound * t_bound <= NORM_LIMIT, 1.0, 0.0), (8, 128)
    )

    for copy in waiting:
        copy.wait_send()
    for d in range(1, 16):
        send_row(d).wait_send()
    for step in range(1, 8):
        t, ref = line_ref(step, c)
        remote(ref, ref, t_pass.at[step], t_recv.at[t], partner).wait_send()
    for d in range(1, 16):
        t = lax.rem(t_own + d, 16)
        remote(cout.at[t], cin.at[t], c_send.at[t], c_recv.at[t], partner).wait_send()


def fused(frame_one, frame_two, conv_weight, proj_weight):
    vmem = pl.BlockSpec(memory_space=pltpu.VMEM)
    dma = pltpu.SemaphoreType.DMA
    return pl.pallas_call(
        fused_kernel,
        out_shape=[
            jax.ShapeDtypeStruct((2, 1, 256), F32),
            jax.ShapeDtypeStruct((2, 1, 256), F32),
            jax.ShapeDtypeStruct((8, 128), F32),
        ],
        in_specs=[vmem] * 4,
        out_specs=[vmem] * 3,
        scratch_shapes=[
            pltpu.VMEM((2, 2, 256, 128), BF16),
            pltpu.VMEM((16, 272, 128), BF16),
            pltpu.VMEM((16, 272, 128), BF16),
            pltpu.VMEM((16, 256, 256), BF16),
            pltpu.VMEM((16, 256, 128), F32),
            pltpu.VMEM((16, 256, 128), F32),
            pltpu.VMEM((16, 256, 128), F32),
            pltpu.VMEM((2, 3, 8, 256), F32),
            pltpu.VMEM((16, 8, 128), F32),
            pltpu.VMEM((16, 8, 256), F32),
            pltpu.VMEM((16, 8, 128), F32),
            pltpu.VMEM((16, 8, 256), F32),
            dma((2, 2)), dma((2, 2)),
            dma((2, 16)), dma((2, 16)), dma((8,)), dma((8,)), dma((16,)),
            dma((16,)), dma((16,)), dma((16,)), dma((16,)),
        ],
        compiler_params=pltpu.CompilerParams(
            collective_id=0,
            has_side_effects=True,
            vmem_limit_bytes=48 << 20,
        ),
        name="flow",
    )(frame_one, frame_two, conv_weight, proj_weight)


def padded_2(block, sides, width):
    for axis, dim in sides:
        count = lax.axis_size(axis)
        forward = [(i, i + 1) for i in range(count - 1)]
        backward = [(target, source) for source, target in forward]
        low = lax.ppermute(
            lax.slice_in_dim(block, block.shape[dim] - width, None, axis=dim), axis, forward
        )
        high = lax.ppermute(lax.slice_in_dim(block, 0, width, axis=dim), axis, backward)
        block = jnp.concatenate([low, block, high], axis=dim)
    return block


def gathered(part, axis):
    count = lax.axis_size(axis)
    return lax.all_to_all(jnp.broadcast_to(part[None], (count, *part.shape)), axis, 0, 0)


def merged(value, axis, join):
    count = lax.axis_size(axis)
    pieces = jax.tree.map(lambda part: lax.all_to_all(part.reshape(count, -1), axis, 0, 0), value)
    head = jax.tree.map(lambda part: part[0], pieces)
    tail = jax.tree.map(lambda part: part[1:], pieces)
    subtotal, _ = lax.scan(lambda subtotal, piece: (join(subtotal, piece), None), head, tail)
    return subtotal


def encode(stacked, conv_weight, proj_weight):
    padded = padded_2(stacked, ((("src", "tgt"), 1),), 1)
    padded = jnp.pad(padded, ((0, 0), (0, 0), (1, 1), (0, 0)))
    strip_rows, columns = (stacked.shape[1], stacked.shape[2])
    total = jnp.zeros(stacked.shape, jnp.float32)
    for offset_row in range(3):
        for offset_col in range(3):
            window = padded[
                :, offset_row : offset_row + strip_rows, offset_col : offset_col + columns, :
            ]
            total = total + jnp.dot(
                window, conv_weight[3 * offset_row + offset_col], preferred_element_type=jnp.float32
            )
    hidden = jax.nn.relu(total).astype(jnp.bfloat16)
    mixed = stacked.astype(jnp.float32) + jnp.dot(
        hidden, proj_weight, preferred_element_type=jnp.float32
    )
    return mixed.astype(jnp.bfloat16)


def merge_pair(former, latter):
    highest = jnp.maximum(former[0], latter[0])
    keep_former = jnp.exp(former[0] - highest)
    keep_latter = jnp.exp(latter[0] - highest)
    return (
        highest,
        former[1] * keep_former + latter[1] * keep_latter,
        former[2] * keep_former + latter[2] * keep_latter,
        former[3] * keep_former + latter[3] * keep_latter,
    )


def tile_stats(piece_block, block_x, block_y, fixed_flat, fixed_x, fixed_y, factor):
    scores = (
        lax.dot_general(
            piece_block, fixed_flat, (((1,), (1,)), ((), ())), preferred_element_type=jnp.float32
        )
        * factor
    )
    row_top = jnp.max(scores, axis=1)
    row_weights = jnp.exp(scores - row_top[:, None])
    row_stats = (
        row_top,
        jnp.sum(row_weights, axis=1),
        jnp.sum(row_weights * fixed_x[None, :], axis=1),
        jnp.sum(row_weights * fixed_y[None, :], axis=1),
    )
    column_top = jnp.max(scores, axis=0)
    column_weights = jnp.exp(scores - column_top[None, :])
    column_stats = (
        column_top,
        jnp.sum(column_weights, axis=0),
        jnp.sum(column_weights * block_x[:, None], axis=0),
        jnp.sum(column_weights * block_y[:, None], axis=0),
    )
    return (row_stats, column_stats)


def general(frame_one, frame_two, conv_weight, proj_weight):
    features = encode(jnp.stack([frame_one, frame_two]), conv_weight, proj_weight)
    source_feat = features[0]
    target_feat = features[1]
    strip_rows, columns, channels = frame_one.shape
    src_index = lax.axis_index("src")
    tgt_index = lax.axis_index("tgt")
    src_count = lax.axis_size("src")
    tgt_count = lax.axis_size("tgt")
    factor = 1.0 / math.sqrt(channels)
    source_pixels = strip_rows * tgt_count * columns
    target_pixels = strip_rows * src_count * columns

    def pixel_coords(row_numbers):
        coord_y = jnp.repeat(row_numbers.astype(jnp.float32), columns)
        coord_x = jnp.tile(jnp.arange(columns, dtype=jnp.float32), row_numbers.shape[0])
        return (coord_x, coord_y)

    def empty_stats(count):
        zeros_line = jnp.zeros((count,), jnp.float32)
        return (jnp.full((count,), -jnp.inf, jnp.float32), zeros_line, zeros_line, zeros_line)

    target_tile = gathered(target_feat, "src").reshape(-1, columns, channels)
    whole_row = jnp.arange(strip_rows * src_count, dtype=jnp.int32)
    tile_x, tile_y = pixel_coords(
        (whole_row // strip_rows * tgt_count + tgt_index) * strip_rows + whole_row % strip_rows
    )
    fixed_flat = target_tile.reshape(-1, channels)
    shard_piece = gathered(source_feat, "tgt").reshape(-1, columns, channels)
    piece_rows = shard_piece.shape[0]
    block_rows = math.gcd(piece_rows, max(1, 512 // columns))
    blocks = piece_rows // block_rows
    block_size = block_rows * columns
    piece_x, piece_y = pixel_coords(
        src_index * tgt_count * strip_rows + jnp.arange(piece_rows, dtype=jnp.int32)
    )

    def block_step(fixed_acc, block_item):
        piece_block, block_x, block_y = block_item
        row_stats, column_stats = tile_stats(
            piece_block, block_x, block_y, fixed_flat, tile_x, tile_y, factor
        )
        return (merge_pair(fixed_acc, column_stats), row_stats)

    fixed_acc, row_parts = lax.scan(
        block_step,
        (empty_stats(target_pixels), empty_stats(source_pixels))[0],
        (
            shard_piece.reshape(blocks, block_size, channels),
            piece_x.reshape(blocks, block_size),
            piece_y.reshape(blocks, block_size),
        ),
    )
    placed = tuple((segment.reshape(-1) for segment in row_parts))
    fixed_acc, piece_acc = (fixed_acc, placed)
    source_stats, target_stats = (piece_acc, fixed_acc)
    own_x, own_y = pixel_coords(
        (src_index * tgt_count + tgt_index) * strip_rows + jnp.arange(strip_rows, dtype=jnp.int32)
    )
    merged_rows = merged(source_stats, "tgt", merge_pair)
    merged_cols = merged(target_stats, "src", merge_pair)
    source_sums = merged_rows[1:]
    target_sums = merged_cols[1:]
    flow_forward = jnp.stack(
        [source_sums[1] / source_sums[0] - own_x, source_sums[2] / source_sums[0] - own_y]
    ).reshape(2, strip_rows, columns)
    flow_backward = jnp.stack(
        [target_sums[1] / target_sums[0] - own_x, target_sums[2] / target_sums[0] - own_y]
    ).reshape(2, strip_rows, columns)
    return (flow_forward, flow_backward)


def on_device(frame_one, frame_two, conv_weight, proj_weight):
    flow_forward, flow_backward, flag = fused(frame_one, frame_two, conv_weight, proj_weight)
    return lax.cond(
        flag[0, 0] > 0.5,
        lambda *_: (flow_forward, flow_backward),
        general,
        frame_one, frame_two, conv_weight, proj_weight,
    )


def solution(mesh):
    in_specs = (P(("src", "tgt"), None, None), P(("src", "tgt"), None, None), P(), P())
    out_specs = (P(None, ("src", "tgt"), None), P(None, ("src", "tgt"), None))
    return jax.shard_map(
        on_device, mesh=mesh, in_specs=in_specs, out_specs=out_specs, check_vma=False
    )
```

```python
import math

import jax
import jax.numpy as jnp
from jax import lax
from jax.experimental import pallas as pl
from jax.experimental.pallas import tpu as pltpu
from jax.sharding import PartitionSpec as P

F32 = jnp.float32
BF16 = jnp.bfloat16
FLAT = pl.DeviceIdType.LOGICAL
LOG2_SCALE = math.log2(math.e) / math.sqrt(128.0)
NORM_LIMIT = (96.0 / LOG2_SCALE) ** 2
WC = 16
CHUNKS = 256 // WC


def fused_kernel(
    f1_ref, f2_ref, cw_ref, pw_ref,
    ff_ref, fb_ref, flag_ref,
    halo, S, T, HL, R, Y, G, CC, rout, cout, rin, cin,
    halo_send, halo_recv, s_send, s_recv, t_send, t_pass, t_recv, r_send, r_recv, c_send, c_recv,
):
    src = lax.axis_index("src")
    tgt = lax.axis_index("tgt")
    z = lax.div(src, 2)
    x = lax.div(tgt, 4)
    c = lax.rem(tgt, 2)
    y = lax.rem(src, 2) * 2 + lax.rem(lax.div(tgt, 2), 2)
    me = src * 16 + tgt

    def x_slots(d):
        return 2 * lax.rem(x + d, 4)

    def y_slots(d):
        row = lax.rem(y + d, 4)
        return 8 * lax.div(row, 2) + lax.rem(row, 2)

    slots_x = [x_slots(d) for d in range(4)]
    slots_y = [y_slots(d) for d in range(4)]
    k_own = slots_x[0] + slots_y[0]
    t_own = z * 2 + c
    plane = z * 32 + c
    line = 2 * k_own
    partner = plane + line + 1 - 2 * c

    def line_z(step):
        return lax.rem(z + 8 + (2 * lax.rem(step, 2) - 1) * lax.div(step + 1, 2), 8)

    up = lax.rem(me + 255, 256)
    down = lax.rem(me + 1, 256)

    barrier = pltpu.get_barrier_semaphore()
    peers = [up, down, partner]
    for d in range(1, 8):
        for pc in range(2):
            peers.append(32 * lax.rem(z + d, 8) + line + pc)
    for d in range(1, 16):
        peers.append(plane + 2 * lax.rem(k_own + d, 16))
    for peer in peers:
        pl.semaphore_signal(barrier, inc=1, device_id=peer, device_id_type=FLAT)
    zero_rows = jnp.zeros((256, 128), F32)

    def clear(k, carry):
        R[k] = zero_rows
        Y[k] = zero_rows
        G[k] = zero_rows
        return carry

    pl.semaphore_wait(barrier, len(peers))

    def remote(source, target, send, recv, peer):
        return pltpu.make_async_remote_copy(
            src_ref=source, dst_ref=target, send_sem=send, recv_sem=recv,
            device_id=peer, device_id_type=FLAT,
        )

    halos = []
    for frame, ref in ((0, f1_ref), (1, f2_ref)):
        halos.append(remote(ref.at[0], halo.at[0, frame], halo_send.at[0, frame], halo_recv.at[0, frame], down))
        halos.append(remote(ref.at[0], halo.at[1, frame], halo_send.at[1, frame], halo_recv.at[1, frame], up))
    for copy in halos:
        copy.start()
    lax.fori_loop(0, 16, clear, 0)
    def encode_row(frame, out, slot):
        def body(main, third):
            column = lax.broadcasted_iota(jnp.int32, (256, 128), 0)
            zero_bf = jnp.zeros((256, 128), BF16)
            zero_tap = jnp.zeros((128, 128), BF16)

            def side(left, right):
                return jnp.concatenate([left, right], axis=1)

            def tap_tile(half, m):
                rows = []
                for a in (0, 1) if half == 0 else (2, 3):
                    tap = [
                        cw_ref[3 * a + b] if a < 3 and b < 3 else zero_tap
                        for b in ((0, 1) if m == 0 else (2, 3))
                    ]
                    rows.append(side(*tap))
                return jnp.concatenate(rows, axis=0)

            own = (f1_ref, f2_ref)[frame][0]
            for half in range(2):
                if half == 0:
                    lhs = side(jnp.where(me > 0, halo[0, frame], zero_bf), own)
                else:
                    lhs = side(jnp.where(me < 255, halo[1, frame], zero_bf), zero_bf)
                for m, acc in ((0, main), (1, third)):
                    pltpu.matmul_push_rhs(tap_tile(half, m), 0, m)
                    pltpu.matmul_acc_lhs(acc, lhs, load_staged_rhs=0)
            pw = jnp.concatenate([side(pw_ref[...], zero_tap), side(zero_tap, zero_tap)], axis=0)
            pltpu.matmul_push_rhs(pw, 0, 0)
            sums = pltpu.matmul_pop(main)
            last = pltpu.matmul_pop(third)
            left = jnp.where(column == 0, 0.0, pltpu.roll(sums[:, 0:128], 1, 0))
            right = jnp.where(column == 255, 0.0, pltpu.roll(last[:, 0:128], 255, 0))
            hidden = jnp.maximum(left + sums[:, 128:256] + right, 0.0).astype(BF16)
            pltpu.matmul_acc_lhs(main, side(hidden, zero_bf), load_staged_rhs=0)
            mixed = pltpu.matmul_pop(main)
            feature = (own.astype(F32) + mixed[:, 0:128]).astype(BF16)
            wide = feature.astype(F32)
            norm = jnp.max(jnp.sum(wide * wide, axis=1, keepdims=True), axis=0, keepdims=True)
            out[slot, 0:16, :] = jnp.broadcast_to(norm * 1.01, (16, 128)).astype(BF16)
            out[slot, 16:272, :] = feature

        for copy in halos[2 * frame : 2 * frame + 2]:
            copy.wait()
        pl.run_scoped(body, pltpu.ACC(0)((256, 256), F32), pltpu.ACC(1)((256, 256), F32))

    parts = (slice(0, 144), slice(144, 272))
    waiting = []
    sent = [0, 0]

    def send_half(half, k, to):
        ref = S.at[k, parts[half]]
        copy = remote(ref, ref, s_send.at[half, sent[half]], s_recv.at[half, k], plane + 2 * to)
        sent[half] += 1
        copy.start()
        waiting.append(copy)

    def split(half, k):
        w = slice(128 * half, 128 * half + 128)
        value = S[k, 16 + 128 * half : 144 + 128 * half, :].astype(F32) * LOG2_SCALE
        head = value.astype(BF16)
        HL[k, w, 0:128] = head
        HL[k, w, 128:256] = (value - head.astype(F32)).astype(BF16)

    def arrive(half, k):
        ref = S.at[k, parts[half]]
        remote(ref, ref, s_send.at[half, 0], s_recv.at[half, k], partner).wait_recv()

    first = (slots_x, slots_y)
    second = (slots_y, slots_x)
    odd_x = lax.rem(x, 2)
    odd_y = lax.rem(y, 2)

    def turned(half, d, flip):
        here = odd_x if half == 0 else odd_y
        odd = here if d % 2 == 0 else 1 - here
        if flip:
            odd = 1 - odd
        return second[half][1] + odd * (second[half][3] - second[half][1])

    encode_row(0, S, k_own)
    for d in (1, 3, 2):
        for half in range(2):
            send_half(half, k_own, first[half][d] + second[half][0])
    for half in range(2):
        for e in (1, 3):
            send_half(half, k_own, first[half][0] + second[half][e])
    encode_row(1, T, t_own)
    own_ref = T.at[t_own]
    copy = remote(own_ref, own_ref, t_send.at[0], t_recv.at[t_own], partner)
    copy.start()
    waiting.append(copy)
    for step in range(1, 8):
        copy = remote(own_ref, own_ref, t_send.at[step], t_recv.at[t_own], 32 * line_z(step) + line + c)
        copy.start()
        waiting.append(copy)
    def forward(d):
        for half in range(2):
            k = first[half][d] + second[half][0]
            arrive(half, k)
            for e in (1, 3, 2):
                send_half(half, k, first[half][0] + second[half][e])

    def relay(d):
        for half in range(2):
            k = first[half][d] + turned(half, d, True)
            arrive(half, k)
            send_half(half, k, first[half][0] + turned(half, d, False))

    for half in range(2):
        send_half(half, k_own, first[half][0] + second[half][2])
    forward(1)
    forward(3)
    forward(2)
    for d in (0, 1, 3, 2):
        for half in range(2):
            arrive(half, first[half][d] + turned(half, d, True))
    for d in (0, 1, 3, 2):
        for half in range(2):
            split(half, first[half][d] + second[half][0])
            split(half, first[half][d] + turned(half, d, True))
    for far in (False, True):
        for d in (0, 1, 3, 2):
            for half in range(2):
                k = first[half][d] + (second[half][2] if far else turned(half, d, False))
                arrive(half, k)
                split(half, k)

    def line_ref(step, pc):
        t = line_z(step) * 2 + pc
        return t, T.at[t]

    def pass_on(step):
        t, ref = line_ref(step, c)
        remote(ref, ref, t_send.at[0], t_recv.at[t], partner).wait_recv()
        remote(ref, ref, t_pass.at[step], t_recv.at[t], partner).start()

    def passed(step):
        t, ref = line_ref(step, 1 - c)
        remote(ref, ref, t_send.at[0], t_recv.at[t], partner).wait_recv()

    def largest(rows):
        return jnp.max(jnp.max(rows, axis=0)[0:8], axis=(0, 1), keepdims=True)

    s_norm = jnp.broadcast_to(largest(S[:, 0:16, :].astype(F32)), (1, 256))

    base_rows = line.astype(F32)
    base_cols = plane.astype(F32)

    def send_column(zt, m):
        t = 2 * zt + m

        @pl.when(t != t_own)
        def _():
            remote(
                cout.at[t], cin.at[t_own], c_send.at[t], c_recv.at[t_own], 32 * zt + line + m
            ).start()

        @pl.when(t == t_own)
        def _():
            cin[t] = cout[t]

    def tile(*accs):
        slots = ((accs[0:16], accs[16:32]), (accs[32:48], accs[48:64]))

        def push(zt):
            for m in range(2):
                w = T[2 * zt + m, 16:272, :]
                pltpu.matmul_push_rhs(jnp.concatenate([w, w], axis=1), 0, m, transpose=True)

        def issue(slot, chunk, load):
            for k in range(15, -1, -1):
                lhs = HL[k, pl.ds(chunk * WC, WC), :]
                for m in range(2):
                    pltpu.matmul_acc_lhs(
                        slots[slot][m][k], lhs, load_staged_rhs=0 if load and k == 15 else None
                    )

        def process(slot, chunk, row_weight):
            window = pl.ds(chunk * WC, WC)
            total = [None, None]
            ranked = [None, None]
            for k in range(15, -1, -1):
                e = [jnp.exp2(pltpu.matmul_pop(slots[slot][m][k])) for m in range(2)]
                odd = e[1][:, :128] + e[1][:, 128:]
                both = odd + (e[0][:, :128] + e[0][:, 128:])
                R[k, window, :] = R[k, window, :] + both
                Y[k, window, :] = Y[k, window, :] + (both * row_weight + odd)
                G[k, window, :] = G[k, window, :] + (e[1][:, 128:] + e[0][:, 128:])
                for m in range(2):
                    total[m] = e[m] if k == 15 else total[m] + e[m]
                    if k == 15:
                        ranked[m] = total[m]
                    elif k > 0:
                        ranked[m] = ranked[m] + total[m]
            weight = (lax.broadcasted_iota(jnp.int32, (WC, 256), 0) + chunk * WC).astype(F32)
            for m in range(2):
                CC[m, 0] += jnp.sum(total[m].reshape(WC // 8, 8, 256), axis=0)
                CC[m, 1] += jnp.sum((total[m] * weight).reshape(WC // 8, 8, 256), axis=0)
                CC[m, 2] += jnp.sum(ranked[m].reshape(WC // 8, 8, 256), axis=0)

        def per_pair(step, carry):
            zt = line_z(step)
            row_weight = (zt * 32).astype(F32)

            @pl.when(step > 0)
            def _():
                for m in range(2):
                    send_column(line_z(step - 1), m)

            @pl.when(step < 6)
            def _():
                pass_on(step + 2)

            CC[...] = jnp.zeros_like(CC)

            def inner(i, inner_carry):
                issue(1, 2 * i + 1, False)
                process(0, 2 * i, row_weight)
                issue(0, 2 * i + 2, False)
                process(1, 2 * i + 1, row_weight)
                return inner_carry

            lax.fori_loop(0, CHUNKS // 2 - 1, inner, 0)

            @pl.when(step < 7)
            def _():
                passed(step + 1)

            issue(1, CHUNKS - 1, False)
            process(0, CHUNKS - 2, row_weight)
            push(line_z(lax.rem(step + 1, 8)))
            issue(0, 0, True)
            process(1, CHUNKS - 1, row_weight)
            for m in range(2):
                count = jnp.sum(CC[m, 0], axis=0, keepdims=True)
                cout[2 * zt + m, 0:1, :] = count
                cout[2 * zt + m, 1:2, :] = jnp.sum(CC[m, 1], axis=0, keepdims=True)
                cout[2 * zt + m, 2:3, :] = (
                    2.0 * jnp.sum(CC[m, 2], axis=0, keepdims=True) + base_cols * count
                )
                cout[2 * zt + m, 3:4, :] = s_norm
            return carry

        passed(0)
        pass_on(1)
        push(line_z(0))
        issue(0, 0, True)
        lax.fori_loop(0, 8, per_pair, 0)
        for k in range(16):
            for m in range(2):
                CC[m, 0] = pltpu.matmul_pop(slots[0][m][k])[:8]

    pl.run_scoped(
        tile, *[pltpu.ACC(m)((WC, 256), F32) for m in (0, 1, 0, 1) for _ in range(16)]
    )

    lane = lax.broadcasted_iota(jnp.int32, (8, 128), 1)
    lane_weight = lane.astype(F32)
    t_norm = jnp.broadcast_to(largest(T[:, 0:16, :].astype(F32)), (8, 128))

    for m in range(2):
        send_column(line_z(7), m)

    def finish(k):
        packed = [t_norm, t_norm, t_norm]
        for g in range(32):
            w = slice(8 * g, 8 * g + 8)
            r = R[k, w, :]
            for i, value in enumerate((r, r * lane_weight + 128.0 * G[k, w, :], Y[k, w, :])):
                packed[i] = jnp.where(lane == 32 * i + g, jnp.sum(value, axis=1, keepdims=True), packed[i])
        count, col_x, col_y = packed
        col_y = col_y + base_rows * pltpu.roll(count, 64, 1)
        rout[k] = jnp.where(lane < 32, count, jnp.where(lane < 64, col_x, jnp.where(lane < 96, col_y, t_norm)))

    def send_row(k):
        return remote(rout.at[k], rin.at[k_own], r_send.at[k], r_recv.at[k_own], plane + 2 * k)

    def far_slot(i):
        row = lax.rem(y + 2 + lax.rem(i, 4), 4)
        return 2 * lax.rem(x + 2 + lax.div(i, 4), 4) + 8 * lax.div(row, 2) + lax.rem(row, 2)

    def hand_out(k):
        @pl.when(k != k_own)
        def _():
            send_row(k).start()

        @pl.when(k == k_own)
        def _():
            rin[k] = rout[k]

    def two_rows(i, carry):
        pair = (far_slot(2 * i), far_slot(2 * i + 1))
        for k in pair:
            finish(k)

        @pl.when(i > 0)
        def _():
            for k in carry:
                hand_out(k)

        return pair

    for k in lax.fori_loop(0, 8, two_rows, (k_own, k_own)):
        hand_out(k)
    for copy in waiting:
        copy.wait_send()
    for step in range(1, 8):
        t, ref = line_ref(step, c)
        remote(ref, ref, t_pass.at[step], t_recv.at[t], partner).wait_send()

    for d in range(1, 16):
        t = lax.rem(t_own + d, 16)
        remote(cout.at[t], cin.at[t], c_send.at[t], c_recv.at[t], partner).wait_recv()
    merged = jnp.sum(cin[...], axis=0)
    coord_x = lax.broadcasted_iota(jnp.int32, (1, 256), 1).astype(F32)
    coord_y = me.astype(F32)
    fb_ref[0, 0:1, :] = merged[1:2] / merged[0:1] - coord_x
    fb_ref[1, 0:1, :] = merged[2:3] / merged[0:1] - coord_y
    s_bound = jnp.max(jnp.max(cin[...], axis=0)[3:4, 0:128], axis=1, keepdims=True)
    for d in range(1, 16):
        send_row(lax.rem(k_own + d, 16)).wait_send()
    for d in range(1, 16):
        t = lax.rem(t_own + d, 16)
        remote(cout.at[t], cin.at[t], c_send.at[t], c_recv.at[t], partner).wait_send()
    for d in range(1, 16):
        k = lax.rem(k_own + d, 16)
        remote(rout.at[k], rin.at[k], r_send.at[k], r_recv.at[k], partner).wait_recv()
    sums = jnp.sum(rin[...], axis=0)
    sublane = lax.broadcasted_iota(jnp.int32, (8, 128), 0)
    flows = (
        pltpu.roll(sums, 96, 1) / sums - (lane * 8 + sublane).astype(F32),
        pltpu.roll(sums, 64, 1) / sums - coord_y,
    )
    for i, value in enumerate(flows):
        for h in range(2):
            spread = jnp.take_along_axis(value, 16 * h + lane // 8, axis=1)
            ff_ref[i, 0:1, 128 * h : 128 * h + 128] = jnp.sum(
                jnp.where(sublane == lane % 8, spread, 0.0), axis=0, keepdims=True
            )
    t_bound = jnp.max(
        jnp.where(lane >= 96, jnp.max(rin[...], axis=0), 0.0), axis=(0, 1), keepdims=True
    )
    flag_ref[...] = jnp.where(s_bound * t_bound <= NORM_LIMIT, 1.0, 0.0)


def fused(frame_one, frame_two, conv_weight, proj_weight):
    vmem = pl.BlockSpec(memory_space=pltpu.VMEM)
    dma = pltpu.SemaphoreType.DMA
    return pl.pallas_call(
        fused_kernel,
        out_shape=[
            jax.ShapeDtypeStruct((2, 1, 256), F32),
            jax.ShapeDtypeStruct((2, 1, 256), F32),
            jax.ShapeDtypeStruct((1, 1), F32),
        ],
        in_specs=[vmem] * 4,
        out_specs=[vmem] * 3,
        scratch_shapes=[
            pltpu.VMEM((2, 2, 256, 128), BF16),
            pltpu.VMEM((16, 272, 128), BF16),
            pltpu.VMEM((16, 272, 128), BF16),
            pltpu.VMEM((16, 256, 256), BF16),
            pltpu.VMEM((16, 256, 128), F32),
            pltpu.VMEM((16, 256, 128), F32),
            pltpu.VMEM((16, 256, 128), F32),
            pltpu.VMEM((2, 3, 8, 256), F32),
            pltpu.VMEM((16, 8, 128), F32),
            pltpu.VMEM((16, 8, 256), F32),
            pltpu.VMEM((16, 8, 128), F32),
            pltpu.VMEM((16, 8, 256), F32),
            dma((2, 2)), dma((2, 2)),
            dma((2, 24)), dma((2, 16)), dma((8,)), dma((8,)), dma((16,)),
            dma((16,)), dma((16,)), dma((16,)), dma((16,)),
        ],
        compiler_params=pltpu.CompilerParams(
            collective_id=0,
            has_side_effects=True,
            vmem_limit_bytes=48 << 20,
        ),
        name="flow",
    )(frame_one, frame_two, conv_weight, proj_weight)


def padded_2(block, sides, width):
    for axis, dim in sides:
        count = lax.axis_size(axis)
        forward = [(i, i + 1) for i in range(count - 1)]
        backward = [(target, source) for source, target in forward]
        low = lax.ppermute(
            lax.slice_in_dim(block, block.shape[dim] - width, None, axis=dim), axis, forward
        )
        high = lax.ppermute(lax.slice_in_dim(block, 0, width, axis=dim), axis, backward)
        block = jnp.concatenate([low, block, high], axis=dim)
    return block


def gathered(part, axis):
    count = lax.axis_size(axis)
    return lax.all_to_all(jnp.broadcast_to(part[None], (count, *part.shape)), axis, 0, 0)


def merged(value, axis, join):
    count = lax.axis_size(axis)
    pieces = jax.tree.map(lambda part: lax.all_to_all(part.reshape(count, -1), axis, 0, 0), value)
    head = jax.tree.map(lambda part: part[0], pieces)
    tail = jax.tree.map(lambda part: part[1:], pieces)
    subtotal, _ = lax.scan(lambda subtotal, piece: (join(subtotal, piece), None), head, tail)
    return subtotal


def encode(stacked, conv_weight, proj_weight):
    padded = padded_2(stacked, ((("src", "tgt"), 1),), 1)
    padded = jnp.pad(padded, ((0, 0), (0, 0), (1, 1), (0, 0)))
    strip_rows, columns = (stacked.shape[1], stacked.shape[2])
    total = jnp.zeros(stacked.shape, jnp.float32)
    for offset_row in range(3):
        for offset_col in range(3):
            window = padded[
                :, offset_row : offset_row + strip_rows, offset_col : offset_col + columns, :
            ]
            total = total + jnp.dot(
                window, conv_weight[3 * offset_row + offset_col], preferred_element_type=jnp.float32
            )
    hidden = jax.nn.relu(total).astype(jnp.bfloat16)
    mixed = stacked.astype(jnp.float32) + jnp.dot(
        hidden, proj_weight, preferred_element_type=jnp.float32
    )
    return mixed.astype(jnp.bfloat16)


def merge_pair(former, latter):
    highest = jnp.maximum(former[0], latter[0])
    keep_former = jnp.exp(former[0] - highest)
    keep_latter = jnp.exp(latter[0] - highest)
    return (
        highest,
        former[1] * keep_former + latter[1] * keep_latter,
        former[2] * keep_former + latter[2] * keep_latter,
        former[3] * keep_former + latter[3] * keep_latter,
    )


def tile_stats(piece_block, block_x, block_y, fixed_flat, fixed_x, fixed_y, factor):
    scores = (
        lax.dot_general(
            piece_block, fixed_flat, (((1,), (1,)), ((), ())), preferred_element_type=jnp.float32
        )
        * factor
    )
    row_top = jnp.max(scores, axis=1)
    row_weights = jnp.exp(scores - row_top[:, None])
    row_stats = (
        row_top,
        jnp.sum(row_weights, axis=1),
        jnp.sum(row_weights * fixed_x[None, :], axis=1),
        jnp.sum(row_weights * fixed_y[None, :], axis=1),
    )
    column_top = jnp.max(scores, axis=0)
    column_weights = jnp.exp(scores - column_top[None, :])
    column_stats = (
        column_top,
        jnp.sum(column_weights, axis=0),
        jnp.sum(column_weights * block_x[:, None], axis=0),
        jnp.sum(column_weights * block_y[:, None], axis=0),
    )
    return (row_stats, column_stats)


def general(frame_one, frame_two, conv_weight, proj_weight):
    features = encode(jnp.stack([frame_one, frame_two]), conv_weight, proj_weight)
    source_feat = features[0]
    target_feat = features[1]
    strip_rows, columns, channels = frame_one.shape
    src_index = lax.axis_index("src")
    tgt_index = lax.axis_index("tgt")
    src_count = lax.axis_size("src")
    tgt_count = lax.axis_size("tgt")
    factor = 1.0 / math.sqrt(channels)
    source_pixels = strip_rows * tgt_count * columns
    target_pixels = strip_rows * src_count * columns

    def pixel_coords(row_numbers):
        coord_y = jnp.repeat(row_numbers.astype(jnp.float32), columns)
        coord_x = jnp.tile(jnp.arange(columns, dtype=jnp.float32), row_numbers.shape[0])
        return (coord_x, coord_y)

    def empty_stats(count):
        zeros_line = jnp.zeros((count,), jnp.float32)
        return (jnp.full((count,), -jnp.inf, jnp.float32), zeros_line, zeros_line, zeros_line)

    target_tile = gathered(target_feat, "src").reshape(-1, columns, channels)
    whole_row = jnp.arange(strip_rows * src_count, dtype=jnp.int32)
    tile_x, tile_y = pixel_coords(
        (whole_row // strip_rows * tgt_count + tgt_index) * strip_rows + whole_row % strip_rows
    )
    fixed_flat = target_tile.reshape(-1, channels)
    shard_piece = gathered(source_feat, "tgt").reshape(-1, columns, channels)
    piece_rows = shard_piece.shape[0]
    block_rows = math.gcd(piece_rows, max(1, 512 // columns))
    blocks = piece_rows // block_rows
    block_size = block_rows * columns
    piece_x, piece_y = pixel_coords(
        src_index * tgt_count * strip_rows + jnp.arange(piece_rows, dtype=jnp.int32)
    )

    def block_step(fixed_acc, block_item):
        piece_block, block_x, block_y = block_item
        row_stats, column_stats = tile_stats(
            piece_block, block_x, block_y, fixed_flat, tile_x, tile_y, factor
        )
        return (merge_pair(fixed_acc, column_stats), row_stats)

    fixed_acc, row_parts = lax.scan(
        block_step,
        (empty_stats(target_pixels), empty_stats(source_pixels))[0],
        (
            shard_piece.reshape(blocks, block_size, channels),
            piece_x.reshape(blocks, block_size),
            piece_y.reshape(blocks, block_size),
        ),
    )
    placed = tuple((segment.reshape(-1) for segment in row_parts))
    fixed_acc, piece_acc = (fixed_acc, placed)
    source_stats, target_stats = (piece_acc, fixed_acc)
    own_x, own_y = pixel_coords(
        (src_index * tgt_count + tgt_index) * strip_rows + jnp.arange(strip_rows, dtype=jnp.int32)
    )
    merged_rows = merged(source_stats, "tgt", merge_pair)
    merged_cols = merged(target_stats, "src", merge_pair)
    source_sums = merged_rows[1:]
    target_sums = merged_cols[1:]
    flow_forward = jnp.stack(
        [source_sums[1] / source_sums[0] - own_x, source_sums[2] / source_sums[0] - own_y]
    ).reshape(2, strip_rows, columns)
    flow_backward = jnp.stack(
        [target_sums[1] / target_sums[0] - own_x, target_sums[2] / target_sums[0] - own_y]
    ).reshape(2, strip_rows, columns)
    return (flow_forward, flow_backward)


def on_device(frame_one, frame_two, conv_weight, proj_weight):
    flow_forward, flow_backward, flag = fused(frame_one, frame_two, conv_weight, proj_weight)
    return lax.cond(
        flag[0, 0] > 0.5,
        lambda *_: (flow_forward, flow_backward),
        general,
        frame_one, frame_two, conv_weight, proj_weight,
    )


def solution(mesh):
    in_specs = (P(("src", "tgt"), None, None), P(("src", "tgt"), None, None), P(), P())
    out_specs = (P(None, ("src", "tgt"), None), P(None, ("src", "tgt"), None))
    return jax.shard_map(
        on_device, mesh=mesh, in_specs=in_specs, out_specs=out_specs, check_vma=False
    )
```

```python
import math

import jax
import jax.numpy as jnp
from jax import lax
from jax.experimental import pallas as pl
from jax.experimental.pallas import tpu as pltpu
from jax.sharding import PartitionSpec as P

F32 = jnp.float32
BF16 = jnp.bfloat16
FLAT = pl.DeviceIdType.LOGICAL
LOG2_SCALE = math.log2(math.e) / math.sqrt(128.0)
NORM_LIMIT = (96.0 / LOG2_SCALE) ** 2
WC = 16
CHUNKS = 256 // WC


def fused_kernel(
    f1_hbm, f2_hbm, cw_hbm, pw_hbm,
    ff_ref, fb_ref, flag_ref,
    rows, cw_ref, pw_ref, load_sem, halo, S, T, HL, R, Y, G, CC, rout, cout, rin, cin,
    halo_send, halo_recv, s_send, s_recv, t_send, t_pass, t_recv, r_send, r_recv, c_send, c_recv,
):
    loads = [
        pltpu.make_async_copy(f1_hbm.at[0], rows.at[0], load_sem.at[0]),
        pltpu.make_async_copy(f2_hbm.at[0], rows.at[1], load_sem.at[1]),
        pltpu.make_async_copy(cw_hbm, cw_ref, load_sem.at[2]),
        pltpu.make_async_copy(pw_hbm, pw_ref, load_sem.at[3]),
    ]
    for copy in loads:
        copy.start()
    src = lax.axis_index("src")
    tgt = lax.axis_index("tgt")
    z = lax.div(src, 2)
    x = lax.div(tgt, 4)
    c = lax.rem(tgt, 2)
    y = lax.rem(src, 2) * 2 + lax.rem(lax.div(tgt, 2), 2)
    me = src * 16 + tgt

    def x_slots(d):
        return 2 * lax.rem(x + d, 4)

    def y_slots(d):
        row = lax.rem(y + d, 4)
        return 8 * lax.div(row, 2) + lax.rem(row, 2)

    slots_x = [x_slots(d) for d in range(4)]
    slots_y = [y_slots(d) for d in range(4)]
    k_own = slots_x[0] + slots_y[0]
    t_own = z * 2 + c
    plane = z * 32 + c
    line = 2 * k_own
    partner = plane + line + 1 - 2 * c

    def line_z(step):
        return lax.rem(z + 8 + (2 * lax.rem(step, 2) - 1) * lax.div(step + 1, 2), 8)

    up = lax.rem(me + 255, 256)
    down = lax.rem(me + 1, 256)

    barrier = pltpu.get_barrier_semaphore()
    peers = [up, down, partner]
    for d in range(1, 8):
        for pc in range(2):
            peers.append(32 * lax.rem(z + d, 8) + line + pc)
    for d in range(1, 16):
        peers.append(plane + 2 * lax.rem(k_own + d, 16))
    for peer in peers:
        pl.semaphore_signal(barrier, inc=1, device_id=peer, device_id_type=FLAT)
    zero_rows = jnp.zeros((256, 128), F32)

    def clear(k, carry):
        R[k] = zero_rows
        Y[k] = zero_rows
        G[k] = zero_rows
        return carry

    for copy in loads[:2]:
        copy.wait()
    pl.semaphore_wait(barrier, len(peers))

    def remote(source, target, send, recv, peer):
        return pltpu.make_async_remote_copy(
            src_ref=source, dst_ref=target, send_sem=send, recv_sem=recv,
            device_id=peer, device_id_type=FLAT,
        )

    halos = []
    for frame in range(2):
        halos.append(remote(rows.at[frame], halo.at[0, frame], halo_send.at[0, frame], halo_recv.at[0, frame], down))
        halos.append(remote(rows.at[frame], halo.at[1, frame], halo_send.at[1, frame], halo_recv.at[1, frame], up))
    for copy in halos:
        copy.start()
    lax.fori_loop(0, 16, clear, 0)
    for copy in loads[2:]:
        copy.wait()
    def encode_row(frame, out, slot):
        def body(main, third):
            column = lax.broadcasted_iota(jnp.int32, (256, 128), 0)
            zero_bf = jnp.zeros((256, 128), BF16)
            zero_tap = jnp.zeros((128, 128), BF16)

            def side(left, right):
                return jnp.concatenate([left, right], axis=1)

            def tap_tile(half, m):
                rows = []
                for a in (0, 1) if half == 0 else (2, 3):
                    tap = [
                        cw_ref[3 * a + b] if a < 3 and b < 3 else zero_tap
                        for b in ((0, 1) if m == 0 else (2, 3))
                    ]
                    rows.append(side(*tap))
                return jnp.concatenate(rows, axis=0)

            own = rows[frame]
            for half in range(2):
                if half == 0:
                    lhs = side(jnp.where(me > 0, halo[0, frame], zero_bf), own)
                else:
                    lhs = side(jnp.where(me < 255, halo[1, frame], zero_bf), zero_bf)
                for m, acc in ((0, main), (1, third)):
                    pltpu.matmul_push_rhs(tap_tile(half, m), 0, m)
                    pltpu.matmul_acc_lhs(acc, lhs, load_staged_rhs=0)
            pw = jnp.concatenate([side(pw_ref[...], zero_tap), side(zero_tap, zero_tap)], axis=0)
            pltpu.matmul_push_rhs(pw, 0, 0)
            sums = pltpu.matmul_pop(main)
            last = pltpu.matmul_pop(third)
            left = jnp.where(column == 0, 0.0, pltpu.roll(sums[:, 0:128], 1, 0))
            right = jnp.where(column == 255, 0.0, pltpu.roll(last[:, 0:128], 255, 0))
            hidden = jnp.maximum(left + sums[:, 128:256] + right, 0.0).astype(BF16)
            pltpu.matmul_acc_lhs(main, side(hidden, zero_bf), load_staged_rhs=0)
            mixed = pltpu.matmul_pop(main)
            feature = (own.astype(F32) + mixed[:, 0:128]).astype(BF16)
            wide = feature.astype(F32)
            norm = jnp.max(jnp.sum(wide * wide, axis=1, keepdims=True), axis=0, keepdims=True)
            out[slot, 0:16, :] = jnp.broadcast_to(norm * 1.01, (16, 128)).astype(BF16)
            out[slot, 16:272, :] = feature

        for copy in halos[2 * frame : 2 * frame + 2]:
            copy.wait()
        pl.run_scoped(body, pltpu.ACC(0)((256, 256), F32), pltpu.ACC(1)((256, 256), F32))

    parts = (slice(0, 144), slice(144, 272))
    waiting = []
    sent = [0, 0]

    def send_half(half, k, to):
        ref = S.at[k, parts[half]]
        copy = remote(ref, ref, s_send.at[half, sent[half]], s_recv.at[half, k], plane + 2 * to)
        sent[half] += 1
        copy.start()
        waiting.append(copy)

    def split(half, k):
        w = slice(128 * half, 128 * half + 128)
        value = S[k, 16 + 128 * half : 144 + 128 * half, :].astype(F32) * LOG2_SCALE
        head = value.astype(BF16)
        HL[k, w, 0:128] = head
        HL[k, w, 128:256] = (value - head.astype(F32)).astype(BF16)

    def arrive(half, k):
        ref = S.at[k, parts[half]]
        remote(ref, ref, s_send.at[half, 0], s_recv.at[half, k], partner).wait_recv()

    first = (slots_x, slots_y)
    second = (slots_y, slots_x)
    odd_x = lax.rem(x, 2)
    odd_y = lax.rem(y, 2)

    def turned(half, d, flip):
        here = odd_x if half == 0 else odd_y
        odd = here if d % 2 == 0 else 1 - here
        if flip:
            odd = 1 - odd
        return second[half][1] + odd * (second[half][3] - second[half][1])

    encode_row(0, S, k_own)
    for d in (1, 3, 2):
        for half in range(2):
            send_half(half, k_own, first[half][d] + second[half][0])
    for half in range(2):
        for e in (1, 3):
            send_half(half, k_own, first[half][0] + second[half][e])
    encode_row(1, T, t_own)
    own_ref = T.at[t_own]
    copy = remote(own_ref, own_ref, t_send.at[0], t_recv.at[t_own], partner)
    copy.start()
    waiting.append(copy)
    for step in range(1, 8):
        copy = remote(own_ref, own_ref, t_send.at[step], t_recv.at[t_own], 32 * line_z(step) + line + c)
        copy.start()
        waiting.append(copy)
    def forward(d):
        for half in range(2):
            k = first[half][d] + second[half][0]
            arrive(half, k)
            for e in (1, 3, 2):
                send_half(half, k, first[half][0] + second[half][e])

    def relay(d):
        for half in range(2):
            k = first[half][d] + turned(half, d, True)
            arrive(half, k)
            send_half(half, k, first[half][0] + turned(half, d, False))

    for half in range(2):
        send_half(half, k_own, first[half][0] + second[half][2])
    forward(1)
    forward(3)
    forward(2)
    for d in (0, 1, 3, 2):
        for half in range(2):
            arrive(half, first[half][d] + turned(half, d, True))
    for d in (0, 1, 3, 2):
        for half in range(2):
            split(half, first[half][d] + second[half][0])
            split(half, first[half][d] + turned(half, d, True))
    for far in (False, True):
        for d in (0, 1, 3, 2):
            for half in range(2):
                k = first[half][d] + (second[half][2] if far else turned(half, d, False))
                arrive(half, k)
                split(half, k)

    def line_ref(step, pc):
        t = line_z(step) * 2 + pc
        return t, T.at[t]

    def pass_on(step):
        t, ref = line_ref(step, c)
        remote(ref, ref, t_send.at[0], t_recv.at[t], partner).wait_recv()
        remote(ref, ref, t_pass.at[step], t_recv.at[t], partner).start()

    def passed(step):
        t, ref = line_ref(step, 1 - c)
        remote(ref, ref, t_send.at[0], t_recv.at[t], partner).wait_recv()

    def largest(rows):
        return jnp.max(jnp.max(rows, axis=0)[0:8], axis=(0, 1), keepdims=True)

    s_norm = jnp.broadcast_to(largest(S[:, 0:16, :].astype(F32)), (1, 256))

    base_rows = line.astype(F32)
    base_cols = plane.astype(F32)

    def send_column(zt, m):
        t = 2 * zt + m

        @pl.when(t != t_own)
        def _():
            remote(
                cout.at[t], cin.at[t_own], c_send.at[t], c_recv.at[t_own], 32 * zt + line + m
            ).start()

        @pl.when(t == t_own)
        def _():
            cin[t] = cout[t]

    def tile(*accs):
        slots = ((accs[0:16], accs[16:32]), (accs[32:48], accs[48:64]))

        def push(zt):
            for m in range(2):
                w = T[2 * zt + m, 16:272, :]
                pltpu.matmul_push_rhs(jnp.concatenate([w, w], axis=1), 0, m, transpose=True)

        def issue(slot, chunk, load):
            for k in range(15, -1, -1):
                lhs = HL[k, pl.ds(chunk * WC, WC), :]
                for m in range(2):
                    pltpu.matmul_acc_lhs(
                        slots[slot][m][k], lhs, load_staged_rhs=0 if load and k == 15 else None
                    )

        def process(slot, chunk, row_weight):
            window = pl.ds(chunk * WC, WC)
            total = [None, None]
            ranked = [None, None]
            for k in range(15, -1, -1):
                e = [jnp.exp2(pltpu.matmul_pop(slots[slot][m][k])) for m in range(2)]
                odd = e[1][:, :128] + e[1][:, 128:]
                both = odd + (e[0][:, :128] + e[0][:, 128:])
                R[k, window, :] = R[k, window, :] + both
                Y[k, window, :] = Y[k, window, :] + (both * row_weight + odd)
                G[k, window, :] = G[k, window, :] + (e[1][:, 128:] + e[0][:, 128:])
                for m in range(2):
                    total[m] = e[m] if k == 15 else total[m] + e[m]
                    if k == 15:
                        ranked[m] = total[m]
                    elif k > 0:
                        ranked[m] = ranked[m] + total[m]
            weight = (lax.broadcasted_iota(jnp.int32, (WC, 256), 0) + chunk * WC).astype(F32)
            for m in range(2):
                CC[m, 0] += jnp.sum(total[m].reshape(WC // 8, 8, 256), axis=0)
                CC[m, 1] += jnp.sum((total[m] * weight).reshape(WC // 8, 8, 256), axis=0)
                CC[m, 2] += jnp.sum(ranked[m].reshape(WC // 8, 8, 256), axis=0)

        def per_pair(step, carry):
            zt = line_z(step)
            row_weight = (zt * 32).astype(F32)

            @pl.when(step > 0)
            def _():
                for m in range(2):
                    send_column(line_z(step - 1), m)

            @pl.when(step < 6)
            def _():
                pass_on(step + 2)

            CC[...] = jnp.zeros_like(CC)

            def inner(i, inner_carry):
                issue(1, 2 * i + 1, False)
                process(0, 2 * i, row_weight)
                issue(0, 2 * i + 2, False)
                process(1, 2 * i + 1, row_weight)
                return inner_carry

            lax.fori_loop(0, CHUNKS // 2 - 1, inner, 0)

            @pl.when(step < 7)
            def _():
                passed(step + 1)

            issue(1, CHUNKS - 1, False)
            process(0, CHUNKS - 2, row_weight)
            push(line_z(lax.rem(step + 1, 8)))
            issue(0, 0, True)
            process(1, CHUNKS - 1, row_weight)
            for m in range(2):
                count = jnp.sum(CC[m, 0], axis=0, keepdims=True)
                cout[2 * zt + m, 0:1, :] = count
                cout[2 * zt + m, 1:2, :] = jnp.sum(CC[m, 1], axis=0, keepdims=True)
                cout[2 * zt + m, 2:3, :] = (
                    2.0 * jnp.sum(CC[m, 2], axis=0, keepdims=True) + base_cols * count
                )
                cout[2 * zt + m, 3:4, :] = s_norm
            return carry

        passed(0)
        pass_on(1)
        push(line_z(0))
        issue(0, 0, True)
        lax.fori_loop(0, 8, per_pair, 0)
        for k in range(16):
            for m in range(2):
                CC[m, 0] = pltpu.matmul_pop(slots[0][m][k])[:8]

    pl.run_scoped(
        tile, *[pltpu.ACC(m)((WC, 256), F32) for m in (0, 1, 0, 1) for _ in range(16)]
    )

    lane = lax.broadcasted_iota(jnp.int32, (8, 128), 1)
    lane_weight = lane.astype(F32)
    t_norm = jnp.broadcast_to(largest(T[:, 0:16, :].astype(F32)), (8, 128))

    for m in range(2):
        send_column(line_z(7), m)

    def finish(k):
        packed = [t_norm, t_norm, t_norm]
        for g in range(32):
            w = slice(8 * g, 8 * g + 8)
            r = R[k, w, :]
            for i, value in enumerate((r, r * lane_weight + 128.0 * G[k, w, :], Y[k, w, :])):
                packed[i] = jnp.where(lane == 32 * i + g, jnp.sum(value, axis=1, keepdims=True), packed[i])
        count, col_x, col_y = packed
        col_y = col_y + base_rows * pltpu.roll(count, 64, 1)
        rout[k] = jnp.where(lane < 32, count, jnp.where(lane < 64, col_x, jnp.where(lane < 96, col_y, t_norm)))

    def send_row(k):
        return remote(rout.at[k], rin.at[k_own], r_send.at[k], r_recv.at[k_own], plane + 2 * k)

    def far_slot(i):
        row = lax.rem(y + 2 + lax.rem(i, 4), 4)
        return 2 * lax.rem(x + 2 + lax.div(i, 4), 4) + 8 * lax.div(row, 2) + lax.rem(row, 2)

    def hand_out(k):
        @pl.when(k != k_own)
        def _():
            send_row(k).start()

        @pl.when(k == k_own)
        def _():
            rin[k] = rout[k]

    def two_rows(i, carry):
        pair = (far_slot(2 * i), far_slot(2 * i + 1))
        for k in pair:
            finish(k)

        @pl.when(i > 0)
        def _():
            for k in carry:
                hand_out(k)

        return pair

    for k in lax.fori_loop(0, 8, two_rows, (k_own, k_own)):
        hand_out(k)
    for copy in waiting:
        copy.wait_send()
    for step in range(1, 8):
        t, ref = line_ref(step, c)
        remote(ref, ref, t_pass.at[step], t_recv.at[t], partner).wait_send()

    for d in range(1, 16):
        t = lax.rem(t_own + d, 16)
        remote(cout.at[t], cin.at[t], c_send.at[t], c_recv.at[t], partner).wait_recv()
    merged = jnp.sum(cin[...], axis=0)
    coord_x = lax.broadcasted_iota(jnp.int32, (1, 256), 1).astype(F32)
    coord_y = me.astype(F32)
    fb_ref[0, 0:1, :] = merged[1:2] / merged[0:1] - coord_x
    fb_ref[1, 0:1, :] = merged[2:3] / merged[0:1] - coord_y
    s_bound = jnp.max(jnp.max(cin[...], axis=0)[3:4, 0:128], axis=1, keepdims=True)
    for d in range(1, 16):
        send_row(lax.rem(k_own + d, 16)).wait_send()
    for d in range(1, 16):
        t = lax.rem(t_own + d, 16)
        remote(cout.at[t], cin.at[t], c_send.at[t], c_recv.at[t], partner).wait_send()
    for d in range(1, 16):
        k = lax.rem(k_own + d, 16)
        remote(rout.at[k], rin.at[k], r_send.at[k], r_recv.at[k], partner).wait_recv()
    sums = jnp.sum(rin[...], axis=0)
    sublane = lax.broadcasted_iota(jnp.int32, (8, 128), 0)
    flows = (
        pltpu.roll(sums, 96, 1) / sums - (lane * 8 + sublane).astype(F32),
        pltpu.roll(sums, 64, 1) / sums - coord_y,
    )
    for i, value in enumerate(flows):
        for h in range(2):
            spread = jnp.take_along_axis(value, 16 * h + lane // 8, axis=1)
            ff_ref[i, 0:1, 128 * h : 128 * h + 128] = jnp.sum(
                jnp.where(sublane == lane % 8, spread, 0.0), axis=0, keepdims=True
            )
    t_bound = jnp.max(
        jnp.where(lane >= 96, jnp.max(rin[...], axis=0), 0.0), axis=(0, 1), keepdims=True
    )
    flag_ref[...] = jnp.where(s_bound * t_bound <= NORM_LIMIT, 1.0, 0.0)


def fused(frame_one, frame_two, conv_weight, proj_weight):
    vmem = pl.BlockSpec(memory_space=pltpu.VMEM)
    dma = pltpu.SemaphoreType.DMA
    return pl.pallas_call(
        fused_kernel,
        out_shape=[
            jax.ShapeDtypeStruct((2, 1, 256), F32),
            jax.ShapeDtypeStruct((2, 1, 256), F32),
            jax.ShapeDtypeStruct((1, 1), F32),
        ],
        in_specs=[pl.BlockSpec(memory_space=pltpu.HBM)] * 4,
        out_specs=[vmem] * 3,
        scratch_shapes=[
            pltpu.VMEM((2, 256, 128), BF16),
            pltpu.VMEM((9, 128, 128), BF16),
            pltpu.VMEM((128, 128), BF16),
            dma((4,)),
            pltpu.VMEM((2, 2, 256, 128), BF16),
            pltpu.VMEM((16, 272, 128), BF16),
            pltpu.VMEM((16, 272, 128), BF16),
            pltpu.VMEM((16, 256, 256), BF16),
            pltpu.VMEM((16, 256, 128), F32),
            pltpu.VMEM((16, 256, 128), F32),
            pltpu.VMEM((16, 256, 128), F32),
            pltpu.VMEM((2, 3, 8, 256), F32),
            pltpu.VMEM((16, 8, 128), F32),
            pltpu.VMEM((16, 8, 256), F32),
            pltpu.VMEM((16, 8, 128), F32),
            pltpu.VMEM((16, 8, 256), F32),
            dma((2, 2)), dma((2, 2)),
            dma((2, 24)), dma((2, 16)), dma((8,)), dma((8,)), dma((16,)),
            dma((16,)), dma((16,)), dma((16,)), dma((16,)),
        ],
        compiler_params=pltpu.CompilerParams(
            collective_id=0,
            has_side_effects=True,
            vmem_limit_bytes=48 << 20,
        ),
        name="flow",
    )(frame_one, frame_two, conv_weight, proj_weight)


def padded_2(block, sides, width):
    for axis, dim in sides:
        count = lax.axis_size(axis)
        forward = [(i, i + 1) for i in range(count - 1)]
        backward = [(target, source) for source, target in forward]
        low = lax.ppermute(
            lax.slice_in_dim(block, block.shape[dim] - width, None, axis=dim), axis, forward
        )
        high = lax.ppermute(lax.slice_in_dim(block, 0, width, axis=dim), axis, backward)
        block = jnp.concatenate([low, block, high], axis=dim)
    return block


def gathered(part, axis):
    count = lax.axis_size(axis)
    return lax.all_to_all(jnp.broadcast_to(part[None], (count, *part.shape)), axis, 0, 0)


def merged(value, axis, join):
    count = lax.axis_size(axis)
    pieces = jax.tree.map(lambda part: lax.all_to_all(part.reshape(count, -1), axis, 0, 0), value)
    head = jax.tree.map(lambda part: part[0], pieces)
    tail = jax.tree.map(lambda part: part[1:], pieces)
    subtotal, _ = lax.scan(lambda subtotal, piece: (join(subtotal, piece), None), head, tail)
    return subtotal


def encode(stacked, conv_weight, proj_weight):
    padded = padded_2(stacked, ((("src", "tgt"), 1),), 1)
    padded = jnp.pad(padded, ((0, 0), (0, 0), (1, 1), (0, 0)))
    strip_rows, columns = (stacked.shape[1], stacked.shape[2])
    total = jnp.zeros(stacked.shape, jnp.float32)
    for offset_row in range(3):
        for offset_col in range(3):
            window = padded[
                :, offset_row : offset_row + strip_rows, offset_col : offset_col + columns, :
            ]
            total = total + jnp.dot(
                window, conv_weight[3 * offset_row + offset_col], preferred_element_type=jnp.float32
            )
    hidden = jax.nn.relu(total).astype(jnp.bfloat16)
    mixed = stacked.astype(jnp.float32) + jnp.dot(
        hidden, proj_weight, preferred_element_type=jnp.float32
    )
    return mixed.astype(jnp.bfloat16)


def merge_pair(former, latter):
    highest = jnp.maximum(former[0], latter[0])
    keep_former = jnp.exp(former[0] - highest)
    keep_latter = jnp.exp(latter[0] - highest)
    return (
        highest,
        former[1] * keep_former + latter[1] * keep_latter,
        former[2] * keep_former + latter[2] * keep_latter,
        former[3] * keep_former + latter[3] * keep_latter,
    )


def tile_stats(piece_block, block_x, block_y, fixed_flat, fixed_x, fixed_y, factor):
    scores = (
        lax.dot_general(
            piece_block, fixed_flat, (((1,), (1,)), ((), ())), preferred_element_type=jnp.float32
        )
        * factor
    )
    row_top = jnp.max(scores, axis=1)
    row_weights = jnp.exp(scores - row_top[:, None])
    row_stats = (
        row_top,
        jnp.sum(row_weights, axis=1),
        jnp.sum(row_weights * fixed_x[None, :], axis=1),
        jnp.sum(row_weights * fixed_y[None, :], axis=1),
    )
    column_top = jnp.max(scores, axis=0)
    column_weights = jnp.exp(scores - column_top[None, :])
    column_stats = (
        column_top,
        jnp.sum(column_weights, axis=0),
        jnp.sum(column_weights * block_x[:, None], axis=0),
        jnp.sum(column_weights * block_y[:, None], axis=0),
    )
    return (row_stats, column_stats)


def general(frame_one, frame_two, conv_weight, proj_weight):
    features = encode(jnp.stack([frame_one, frame_two]), conv_weight, proj_weight)
    source_feat = features[0]
    target_feat = features[1]
    strip_rows, columns, channels = frame_one.shape
    src_index = lax.axis_index("src")
    tgt_index = lax.axis_index("tgt")
    src_count = lax.axis_size("src")
    tgt_count = lax.axis_size("tgt")
    factor = 1.0 / math.sqrt(channels)
    source_pixels = strip_rows * tgt_count * columns
    target_pixels = strip_rows * src_count * columns

    def pixel_coords(row_numbers):
        coord_y = jnp.repeat(row_numbers.astype(jnp.float32), columns)
        coord_x = jnp.tile(jnp.arange(columns, dtype=jnp.float32), row_numbers.shape[0])
        return (coord_x, coord_y)

    def empty_stats(count):
        zeros_line = jnp.zeros((count,), jnp.float32)
        return (jnp.full((count,), -jnp.inf, jnp.float32), zeros_line, zeros_line, zeros_line)

    target_tile = gathered(target_feat, "src").reshape(-1, columns, channels)
    whole_row = jnp.arange(strip_rows * src_count, dtype=jnp.int32)
    tile_x, tile_y = pixel_coords(
        (whole_row // strip_rows * tgt_count + tgt_index) * strip_rows + whole_row % strip_rows
    )
    fixed_flat = target_tile.reshape(-1, channels)
    shard_piece = gathered(source_feat, "tgt").reshape(-1, columns, channels)
    piece_rows = shard_piece.shape[0]
    block_rows = math.gcd(piece_rows, max(1, 512 // columns))
    blocks = piece_rows // block_rows
    block_size = block_rows * columns
    piece_x, piece_y = pixel_coords(
        src_index * tgt_count * strip_rows + jnp.arange(piece_rows, dtype=jnp.int32)
    )

    def block_step(fixed_acc, block_item):
        piece_block, block_x, block_y = block_item
        row_stats, column_stats = tile_stats(
            piece_block, block_x, block_y, fixed_flat, tile_x, tile_y, factor
        )
        return (merge_pair(fixed_acc, column_stats), row_stats)

    fixed_acc, row_parts = lax.scan(
        block_step,
        (empty_stats(target_pixels), empty_stats(source_pixels))[0],
        (
            shard_piece.reshape(blocks, block_size, channels),
            piece_x.reshape(blocks, block_size),
            piece_y.reshape(blocks, block_size),
        ),
    )
    placed = tuple((segment.reshape(-1) for segment in row_parts))
    fixed_acc, piece_acc = (fixed_acc, placed)
    source_stats, target_stats = (piece_acc, fixed_acc)
    own_x, own_y = pixel_coords(
        (src_index * tgt_count + tgt_index) * strip_rows + jnp.arange(strip_rows, dtype=jnp.int32)
    )
    merged_rows = merged(source_stats, "tgt", merge_pair)
    merged_cols = merged(target_stats, "src", merge_pair)
    source_sums = merged_rows[1:]
    target_sums = merged_cols[1:]
    flow_forward = jnp.stack(
        [source_sums[1] / source_sums[0] - own_x, source_sums[2] / source_sums[0] - own_y]
    ).reshape(2, strip_rows, columns)
    flow_backward = jnp.stack(
        [target_sums[1] / target_sums[0] - own_x, target_sums[2] / target_sums[0] - own_y]
    ).reshape(2, strip_rows, columns)
    return (flow_forward, flow_backward)


def on_device(frame_one, frame_two, conv_weight, proj_weight):
    flow_forward, flow_backward, flag = fused(frame_one, frame_two, conv_weight, proj_weight)
    return lax.cond(
        flag[0, 0] > 0.5,
        lambda *_: (flow_forward, flow_backward),
        general,
        frame_one, frame_two, conv_weight, proj_weight,
    )


def solution(mesh):
    in_specs = (P(("src", "tgt"), None, None), P(("src", "tgt"), None, None), P(), P())
    out_specs = (P(None, ("src", "tgt"), None), P(None, ("src", "tgt"), None))
    return jax.shard_map(
        on_device, mesh=mesh, in_specs=in_specs, out_specs=out_specs, check_vma=False
    )
```

```python
import math

import jax
import jax.numpy as jnp
from jax import lax
from jax.experimental import pallas as pl
from jax.experimental.pallas import tpu as pltpu
from jax.sharding import PartitionSpec as P

F32 = jnp.float32
BF16 = jnp.bfloat16
FLAT = pl.DeviceIdType.LOGICAL
LOG2_SCALE = math.log2(math.e) / math.sqrt(128.0)
NORM_LIMIT = (96.0 / LOG2_SCALE) ** 2
WC = 16
CHUNKS = 256 // WC


def fused_kernel(
    f1_hbm, f2_hbm, cw_hbm, pw_hbm,
    ff_ref, fb_ref, flag_ref,
    rows, cw_ref, pw_ref, load_sem, halo, S, T, HL, R, Y, G, CC, rout, cout, rin, cin,
    halo_send, halo_recv, s_send, s_recv, t_send, t_pass, t_recv, r_send, r_recv, c_send, c_recv,
):
    loads = [
        pltpu.make_async_copy(f1_hbm.at[0], rows.at[0], load_sem.at[0]),
        pltpu.make_async_copy(f2_hbm.at[0], rows.at[1], load_sem.at[1]),
        pltpu.make_async_copy(cw_hbm, cw_ref, load_sem.at[2]),
        pltpu.make_async_copy(pw_hbm, pw_ref, load_sem.at[3]),
    ]
    for copy in loads:
        copy.start()
    src = lax.axis_index("src")
    tgt = lax.axis_index("tgt")
    z = lax.div(src, 2)
    x = lax.div(tgt, 4)
    c = lax.rem(tgt, 2)
    y = lax.rem(src, 2) * 2 + lax.rem(lax.div(tgt, 2), 2)
    me = src * 16 + tgt

    def x_slots(d):
        return 2 * lax.rem(x + d, 4)

    def y_slots(d):
        row = lax.rem(y + d, 4)
        return 8 * lax.div(row, 2) + lax.rem(row, 2)

    slots_x = [x_slots(d) for d in range(4)]
    slots_y = [y_slots(d) for d in range(4)]
    k_own = slots_x[0] + slots_y[0]
    t_own = z * 2 + c
    plane = z * 32 + c
    line = 2 * k_own
    partner = plane + line + 1 - 2 * c

    def line_z(step):
        return lax.rem(z + 8 + (2 * lax.rem(step, 2) - 1) * lax.div(step + 1, 2), 8)

    up = lax.rem(me + 255, 256)
    down = lax.rem(me + 1, 256)

    barrier = pltpu.get_barrier_semaphore()
    peers = [up, down, partner]
    for d in range(1, 8):
        for pc in range(2):
            peers.append(32 * lax.rem(z + d, 8) + line + pc)
    for d in range(1, 16):
        peers.append(plane + 2 * lax.rem(k_own + d, 16))
    for peer in peers:
        pl.semaphore_signal(barrier, inc=1, device_id=peer, device_id_type=FLAT)
    zero_rows = jnp.zeros((256, 128), F32)

    def clear(k, carry):
        R[k] = zero_rows
        Y[k] = zero_rows
        G[k] = zero_rows
        return carry

    for copy in loads[:2]:
        copy.wait()
    pl.semaphore_wait(barrier, len(peers))

    def remote(source, target, send, recv, peer):
        return pltpu.make_async_remote_copy(
            src_ref=source, dst_ref=target, send_sem=send, recv_sem=recv,
            device_id=peer, device_id_type=FLAT,
        )

    halos = []
    for frame in range(2):
        halos.append(remote(rows.at[frame], halo.at[0, frame], halo_send.at[0, frame], halo_recv.at[0, frame], down))
        halos.append(remote(rows.at[frame], halo.at[1, frame], halo_send.at[1, frame], halo_recv.at[1, frame], up))
    for copy in halos:
        copy.start()
    lax.fori_loop(0, 16, clear, 0)
    for copy in loads[2:]:
        copy.wait()
    def encode_row(frame, out, slot):
        def body(main, third):
            column = lax.broadcasted_iota(jnp.int32, (256, 128), 0)
            zero_bf = jnp.zeros((256, 128), BF16)
            zero_tap = jnp.zeros((128, 128), BF16)

            def side(left, right):
                return jnp.concatenate([left, right], axis=1)

            def tap_tile(half, m):
                rows = []
                for a in (0, 1) if half == 0 else (2, 3):
                    tap = [
                        cw_ref[3 * a + b] if a < 3 and b < 3 else zero_tap
                        for b in ((0, 1) if m == 0 else (2, 3))
                    ]
                    rows.append(side(*tap))
                return jnp.concatenate(rows, axis=0)

            own = rows[frame]
            for half in range(2):
                if half == 0:
                    lhs = side(jnp.where(me > 0, halo[0, frame], zero_bf), own)
                else:
                    lhs = side(jnp.where(me < 255, halo[1, frame], zero_bf), zero_bf)
                for m, acc in ((0, main), (1, third)):
                    pltpu.matmul_push_rhs(tap_tile(half, m), 0, m)
                    pltpu.matmul_acc_lhs(acc, lhs, load_staged_rhs=0)
            pw = jnp.concatenate([side(pw_ref[...], zero_tap), side(zero_tap, zero_tap)], axis=0)
            pltpu.matmul_push_rhs(pw, 0, 0)
            sums = pltpu.matmul_pop(main)
            last = pltpu.matmul_pop(third)
            left = jnp.where(column == 0, 0.0, pltpu.roll(sums[:, 0:128], 1, 0))
            right = jnp.where(column == 255, 0.0, pltpu.roll(last[:, 0:128], 255, 0))
            hidden = jnp.maximum(left + sums[:, 128:256] + right, 0.0).astype(BF16)
            pltpu.matmul_acc_lhs(main, side(hidden, zero_bf), load_staged_rhs=0)
            mixed = pltpu.matmul_pop(main)
            feature = (own.astype(F32) + mixed[:, 0:128]).astype(BF16)
            wide = feature.astype(F32)
            norm = jnp.max(jnp.sum(wide * wide, axis=1, keepdims=True), axis=0, keepdims=True)
            out[slot, 0:16, :] = jnp.broadcast_to(norm * 1.01, (16, 128)).astype(BF16)
            out[slot, 16:272, :] = feature

        for copy in halos[2 * frame : 2 * frame + 2]:
            copy.wait()
        pl.run_scoped(body, pltpu.ACC(0)((256, 256), F32), pltpu.ACC(1)((256, 256), F32))

    parts = (slice(0, 144), slice(144, 272))
    waiting = []
    sent = [0, 0]

    def send_half(half, k, to):
        ref = S.at[k, parts[half]]
        copy = remote(ref, ref, s_send.at[half, sent[half]], s_recv.at[half, k], plane + 2 * to)
        sent[half] += 1
        copy.start()
        waiting.append(copy)

    def split(half, k):
        w = slice(128 * half, 128 * half + 128)
        value = S[k, 16 + 128 * half : 144 + 128 * half, :].astype(F32) * LOG2_SCALE
        head = value.astype(BF16)
        HL[k, w, 0:128] = head
        HL[k, w, 128:256] = (value - head.astype(F32)).astype(BF16)

    def arrive(half, k):
        ref = S.at[k, parts[half]]
        remote(ref, ref, s_send.at[half, 0], s_recv.at[half, k], partner).wait_recv()

    first = (slots_x, slots_y)
    second = (slots_y, slots_x)
    odd_x = lax.rem(x, 2)
    odd_y = lax.rem(y, 2)

    def turned(half, d, flip):
        here = odd_x if half == 0 else odd_y
        odd = here if d % 2 == 0 else 1 - here
        if flip:
            odd = 1 - odd
        return second[half][1] + odd * (second[half][3] - second[half][1])

    encode_row(0, S, k_own)
    for d in (1, 3, 2):
        for half in range(2):
            send_half(half, k_own, first[half][d] + second[half][0])
    for half in range(2):
        for e in (1, 3):
            send_half(half, k_own, first[half][0] + second[half][e])
    encode_row(1, T, t_own)
    own_ref = T.at[t_own]
    copy = remote(own_ref, own_ref, t_send.at[0], t_recv.at[t_own], partner)
    copy.start()
    waiting.append(copy)
    for step in range(1, 8):
        copy = remote(own_ref, own_ref, t_send.at[step], t_recv.at[t_own], 32 * line_z(step) + line + c)
        copy.start()
        waiting.append(copy)
    def forward(d):
        for half in range(2):
            k = first[half][d] + second[half][0]
            arrive(half, k)
            for e in (1, 3, 2):
                send_half(half, k, first[half][0] + second[half][e])

    def relay(d):
        for half in range(2):
            k = first[half][d] + turned(half, d, True)
            arrive(half, k)
            send_half(half, k, first[half][0] + turned(half, d, False))

    for half in range(2):
        send_half(half, k_own, first[half][0] + second[half][2])
    forward(1)
    forward(3)
    forward(2)
    for d in (0, 1, 3, 2):
        for half in range(2):
            arrive(half, first[half][d] + turned(half, d, True))
    for d in (0, 1, 3, 2):
        for half in range(2):
            split(half, first[half][d] + second[half][0])
            split(half, first[half][d] + turned(half, d, True))
    for far in (False, True):
        for d in (0, 1, 3, 2):
            for half in range(2):
                k = first[half][d] + (second[half][2] if far else turned(half, d, False))
                arrive(half, k)
                split(half, k)

    def line_ref(step, pc):
        t = line_z(step) * 2 + pc
        return t, T.at[t]

    def pass_on(step):
        t, ref = line_ref(step, c)
        remote(ref, ref, t_send.at[0], t_recv.at[t], partner).wait_recv()
        remote(ref, ref, t_pass.at[step], t_recv.at[t], partner).start()

    def passed(step):
        t, ref = line_ref(step, 1 - c)
        remote(ref, ref, t_send.at[0], t_recv.at[t], partner).wait_recv()

    def largest(rows):
        return jnp.max(jnp.max(rows, axis=0)[0:8], axis=(0, 1), keepdims=True)

    s_norm = jnp.broadcast_to(largest(S[:, 0:16, :].astype(F32)), (1, 256))

    base_rows = line.astype(F32)
    base_cols = plane.astype(F32)

    def send_column(zt, m):
        t = 2 * zt + m

        @pl.when(t != t_own)
        def _():
            remote(
                cout.at[t], cin.at[t_own], c_send.at[t], c_recv.at[t_own], 32 * zt + line + m
            ).start()

        @pl.when(t == t_own)
        def _():
            cin[t] = cout[t]

    def tile(*accs):
        slots = ((accs[0:16], accs[16:32]), (accs[32:48], accs[48:64]))

        def push(zt):
            for m in range(2):
                w = T[2 * zt + m, 16:272, :]
                pltpu.matmul_push_rhs(jnp.concatenate([w, w], axis=1), 0, m, transpose=True)

        def issue(slot, chunk, load):
            for k in range(15, -1, -1):
                lhs = HL[k, pl.ds(chunk * WC, WC), :]
                for m in range(2):
                    pltpu.matmul_acc_lhs(
                        slots[slot][m][k], lhs, load_staged_rhs=0 if load and k == 15 else None
                    )

        def process(slot, chunk, row_weight):
            window = pl.ds(chunk * WC, WC)
            total = [None, None]
            ranked = [None, None]
            for k in range(15, -1, -1):
                e = [jnp.exp2(pltpu.matmul_pop(slots[slot][m][k])) for m in range(2)]
                odd = e[1][:, :128] + e[1][:, 128:]
                both = odd + (e[0][:, :128] + e[0][:, 128:])
                R[k, window, :] = R[k, window, :] + both
                Y[k, window, :] = Y[k, window, :] + (both * row_weight + odd)
                G[k, window, :] = G[k, window, :] + (e[1][:, 128:] + e[0][:, 128:])
                for m in range(2):
                    total[m] = e[m] if k == 15 else total[m] + e[m]
                    if k == 15:
                        ranked[m] = total[m]
                    elif k > 0:
                        ranked[m] = ranked[m] + total[m]
            weight = (lax.broadcasted_iota(jnp.int32, (WC, 256), 0) + chunk * WC).astype(F32)
            for m in range(2):
                CC[m, 0] += jnp.sum(total[m].reshape(WC // 8, 8, 256), axis=0)
                CC[m, 1] += jnp.sum((total[m] * weight).reshape(WC // 8, 8, 256), axis=0)
                CC[m, 2] += jnp.sum(ranked[m].reshape(WC // 8, 8, 256), axis=0)

        def per_pair(step, carry):
            zt = line_z(step)
            row_weight = (zt * 32).astype(F32)

            @pl.when(step > 0)
            def _():
                for m in range(2):
                    send_column(line_z(step - 1), m)

            @pl.when(step < 6)
            def _():
                pass_on(step + 2)

            CC[...] = jnp.zeros_like(CC)

            def inner(i, inner_carry):
                issue(1, 2 * i + 1, False)
                process(0, 2 * i, row_weight)
                issue(0, 2 * i + 2, False)
                process(1, 2 * i + 1, row_weight)
                return inner_carry

            lax.fori_loop(0, CHUNKS // 2 - 1, inner, 0)

            @pl.when(step < 7)
            def _():
                passed(step + 1)

            issue(1, CHUNKS - 1, False)
            process(0, CHUNKS - 2, row_weight)
            push(line_z(lax.rem(step + 1, 8)))
            issue(0, 0, True)
            process(1, CHUNKS - 1, row_weight)
            for m in range(2):
                count = jnp.sum(CC[m, 0], axis=0, keepdims=True)
                cout[2 * zt + m, 0:1, :] = count
                cout[2 * zt + m, 1:2, :] = jnp.sum(CC[m, 1], axis=0, keepdims=True)
                cout[2 * zt + m, 2:3, :] = (
                    2.0 * jnp.sum(CC[m, 2], axis=0, keepdims=True) + base_cols * count
                )
                cout[2 * zt + m, 3:4, :] = s_norm
            return carry

        passed(0)
        pass_on(1)
        push(line_z(0))
        issue(0, 0, True)
        lax.fori_loop(0, 8, per_pair, 0)
        for k in range(16):
            for m in range(2):
                CC[m, 0] = pltpu.matmul_pop(slots[0][m][k])[:8]

    pl.run_scoped(
        tile, *[pltpu.ACC(m)((WC, 256), F32) for m in (0, 1, 0, 1) for _ in range(16)]
    )

    lane = lax.broadcasted_iota(jnp.int32, (8, 128), 1)
    lane_weight = lane.astype(F32)
    t_norm = jnp.broadcast_to(largest(T[:, 0:16, :].astype(F32)), (8, 128))

    for m in range(2):
        send_column(line_z(7), m)

    def finish(k, accs):
        value = R[k]
        head = value.astype(BF16)
        lhs = jnp.concatenate([head, (value - head.astype(F32)).astype(BF16)], axis=1)
        for m in range(2):
            pltpu.matmul_acc_lhs(accs[m], lhs[128 * m : 128 * m + 128])
        col_x = col_y = t_norm
        for g in range(32):
            w = slice(8 * g, 8 * g + 8)
            first_sum = jnp.sum(R[k, w, :] * lane_weight + 128.0 * G[k, w, :], axis=1, keepdims=True)
            col_x = jnp.where(lane == 32 + g, first_sum, col_x)
            col_y = jnp.where(lane == 64 + g, jnp.sum(Y[k, w, :], axis=1, keepdims=True), col_y)
        counts = [pltpu.matmul_pop(accs[m])[:, 0:128] for m in range(2)]
        count = t_norm
        for g in range(32):
            part = counts[g // 16][8 * (g % 16) : 8 * (g % 16) + 8]
            count = jnp.where(lane % 32 == g, part, count)
        col_y = col_y + base_rows * count
        rout[k] = jnp.where(lane < 32, count, jnp.where(lane < 64, col_x, jnp.where(lane < 96, col_y, t_norm)))

    def send_row(k):
        return remote(rout.at[k], rin.at[k_own], r_send.at[k], r_recv.at[k_own], plane + 2 * k)

    def far_slot(i):
        row = lax.rem(y + 2 + lax.rem(i, 4), 4)
        return 2 * lax.rem(x + 2 + lax.div(i, 4), 4) + 8 * lax.div(row, 2) + lax.rem(row, 2)

    def hand_out(k):
        @pl.when(k != k_own)
        def _():
            send_row(k).start()

        @pl.when(k == k_own)
        def _():
            rin[k] = rout[k]

    def all_rows(*accs):
        for m in range(2):
            pltpu.matmul_push_rhs(jnp.ones((256, 256), BF16), 0, m)
            pltpu.matmul_acc_lhs(accs[m], jnp.zeros((128, 256), BF16), load_staged_rhs=0)
            CC[m, 0] = pltpu.matmul_pop(accs[m])[:8]

        def two_rows(i, carry):
            pair = (far_slot(2 * i), far_slot(2 * i + 1))
            for u, k in enumerate(pair):
                finish(k, accs[2 * u : 2 * u + 2])

            @pl.when(i > 0)
            def _():
                for k in carry:
                    hand_out(k)

            return pair

        for k in lax.fori_loop(0, 8, two_rows, (k_own, k_own)):
            hand_out(k)

    pl.run_scoped(all_rows, *[pltpu.ACC(m)((128, 256), F32) for m in (0, 1, 0, 1)])
    for copy in waiting:
        copy.wait_send()
    for step in range(1, 8):
        t, ref = line_ref(step, c)
        remote(ref, ref, t_pass.at[step], t_recv.at[t], partner).wait_send()

    for d in range(1, 16):
        t = lax.rem(t_own + d, 16)
        remote(cout.at[t], cin.at[t], c_send.at[t], c_recv.at[t], partner).wait_recv()
    merged = jnp.sum(cin[...], axis=0)
    coord_x = lax.broadcasted_iota(jnp.int32, (1, 256), 1).astype(F32)
    coord_y = me.astype(F32)
    fb_ref[0, 0:1, :] = merged[1:2] / merged[0:1] - coord_x
    fb_ref[1, 0:1, :] = merged[2:3] / merged[0:1] - coord_y
    s_bound = jnp.max(jnp.max(cin[...], axis=0)[3:4, 0:128], axis=1, keepdims=True)
    for d in range(1, 16):
        send_row(lax.rem(k_own + d, 16)).wait_send()
    for d in range(1, 16):
        t = lax.rem(t_own + d, 16)
        remote(cout.at[t], cin.at[t], c_send.at[t], c_recv.at[t], partner).wait_send()
    for d in range(1, 16):
        k = lax.rem(k_own + d, 16)
        remote(rout.at[k], rin.at[k], r_send.at[k], r_recv.at[k], partner).wait_recv()
    sums = jnp.sum(rin[...], axis=0)
    sublane = lax.broadcasted_iota(jnp.int32, (8, 128), 0)
    flows = (
        pltpu.roll(sums, 96, 1) / sums - (lane * 8 + sublane).astype(F32),
        pltpu.roll(sums, 64, 1) / sums - coord_y,
    )
    for i, value in enumerate(flows):
        for h in range(2):
            spread = jnp.take_along_axis(value, 16 * h + lane // 8, axis=1)
            ff_ref[i, 0:1, 128 * h : 128 * h + 128] = jnp.sum(
                jnp.where(sublane == lane % 8, spread, 0.0), axis=0, keepdims=True
            )
    t_bound = jnp.max(
        jnp.where(lane >= 96, jnp.max(rin[...], axis=0), 0.0), axis=(0, 1), keepdims=True
    )
    flag_ref[...] = jnp.where(s_bound * t_bound <= NORM_LIMIT, 1.0, 0.0)


def fused(frame_one, frame_two, conv_weight, proj_weight):
    vmem = pl.BlockSpec(memory_space=pltpu.VMEM)
    dma = pltpu.SemaphoreType.DMA
    return pl.pallas_call(
        fused_kernel,
        out_shape=[
            jax.ShapeDtypeStruct((2, 1, 256), F32),
            jax.ShapeDtypeStruct((2, 1, 256), F32),
            jax.ShapeDtypeStruct((1, 1), F32),
        ],
        in_specs=[pl.BlockSpec(memory_space=pltpu.HBM)] * 4,
        out_specs=[vmem] * 3,
        scratch_shapes=[
            pltpu.VMEM((2, 256, 128), BF16),
            pltpu.VMEM((9, 128, 128), BF16),
            pltpu.VMEM((128, 128), BF16),
            dma((4,)),
            pltpu.VMEM((2, 2, 256, 128), BF16),
            pltpu.VMEM((16, 272, 128), BF16),
            pltpu.VMEM((16, 272, 128), BF16),
            pltpu.VMEM((16, 256, 256), BF16),
            pltpu.VMEM((16, 256, 128), F32),
            pltpu.VMEM((16, 256, 128), F32),
            pltpu.VMEM((16, 256, 128), F32),
            pltpu.VMEM((2, 3, 8, 256), F32),
            pltpu.VMEM((16, 8, 128), F32),
            pltpu.VMEM((16, 8, 256), F32),
            pltpu.VMEM((16, 8, 128), F32),
            pltpu.VMEM((16, 8, 256), F32),
            dma((2, 2)), dma((2, 2)),
            dma((2, 24)), dma((2, 16)), dma((8,)), dma((8,)), dma((16,)),
            dma((16,)), dma((16,)), dma((16,)), dma((16,)),
        ],
        compiler_params=pltpu.CompilerParams(
            collective_id=0,
            has_side_effects=True,
            vmem_limit_bytes=48 << 20,
        ),
        name="flow",
    )(frame_one, frame_two, conv_weight, proj_weight)


def padded_2(block, sides, width):
    for axis, dim in sides:
        count = lax.axis_size(axis)
        forward = [(i, i + 1) for i in range(count - 1)]
        backward = [(target, source) for source, target in forward]
        low = lax.ppermute(
            lax.slice_in_dim(block, block.shape[dim] - width, None, axis=dim), axis, forward
        )
        high = lax.ppermute(lax.slice_in_dim(block, 0, width, axis=dim), axis, backward)
        block = jnp.concatenate([low, block, high], axis=dim)
    return block


def gathered(part, axis):
    count = lax.axis_size(axis)
    return lax.all_to_all(jnp.broadcast_to(part[None], (count, *part.shape)), axis, 0, 0)


def merged(value, axis, join):
    count = lax.axis_size(axis)
    pieces = jax.tree.map(lambda part: lax.all_to_all(part.reshape(count, -1), axis, 0, 0), value)
    head = jax.tree.map(lambda part: part[0], pieces)
    tail = jax.tree.map(lambda part: part[1:], pieces)
    subtotal, _ = lax.scan(lambda subtotal, piece: (join(subtotal, piece), None), head, tail)
    return subtotal


def encode(stacked, conv_weight, proj_weight):
    padded = padded_2(stacked, ((("src", "tgt"), 1),), 1)
    padded = jnp.pad(padded, ((0, 0), (0, 0), (1, 1), (0, 0)))
    strip_rows, columns = (stacked.shape[1], stacked.shape[2])
    total = jnp.zeros(stacked.shape, jnp.float32)
    for offset_row in range(3):
        for offset_col in range(3):
            window = padded[
                :, offset_row : offset_row + strip_rows, offset_col : offset_col + columns, :
            ]
            total = total + jnp.dot(
                window, conv_weight[3 * offset_row + offset_col], preferred_element_type=jnp.float32
            )
    hidden = jax.nn.relu(total).astype(jnp.bfloat16)
    mixed = stacked.astype(jnp.float32) + jnp.dot(
        hidden, proj_weight, preferred_element_type=jnp.float32
    )
    return mixed.astype(jnp.bfloat16)


def merge_pair(former, latter):
    highest = jnp.maximum(former[0], latter[0])
    keep_former = jnp.exp(former[0] - highest)
    keep_latter = jnp.exp(latter[0] - highest)
    return (
        highest,
        former[1] * keep_former + latter[1] * keep_latter,
        former[2] * keep_former + latter[2] * keep_latter,
        former[3] * keep_former + latter[3] * keep_latter,
    )


def tile_stats(piece_block, block_x, block_y, fixed_flat, fixed_x, fixed_y, factor):
    scores = (
        lax.dot_general(
            piece_block, fixed_flat, (((1,), (1,)), ((), ())), preferred_element_type=jnp.float32
        )
        * factor
    )
    row_top = jnp.max(scores, axis=1)
    row_weights = jnp.exp(scores - row_top[:, None])
    row_stats = (
        row_top,
        jnp.sum(row_weights, axis=1),
        jnp.sum(row_weights * fixed_x[None, :], axis=1),
        jnp.sum(row_weights * fixed_y[None, :], axis=1),
    )
    column_top = jnp.max(scores, axis=0)
    column_weights = jnp.exp(scores - column_top[None, :])
    column_stats = (
        column_top,
        jnp.sum(column_weights, axis=0),
        jnp.sum(column_weights * block_x[:, None], axis=0),
        jnp.sum(column_weights * block_y[:, None], axis=0),
    )
    return (row_stats, column_stats)


def general(frame_one, frame_two, conv_weight, proj_weight):
    features = encode(jnp.stack([frame_one, frame_two]), conv_weight, proj_weight)
    source_feat = features[0]
    target_feat = features[1]
    strip_rows, columns, channels = frame_one.shape
    src_index = lax.axis_index("src")
    tgt_index = lax.axis_index("tgt")
    src_count = lax.axis_size("src")
    tgt_count = lax.axis_size("tgt")
    factor = 1.0 / math.sqrt(channels)
    source_pixels = strip_rows * tgt_count * columns
    target_pixels = strip_rows * src_count * columns

    def pixel_coords(row_numbers):
        coord_y = jnp.repeat(row_numbers.astype(jnp.float32), columns)
        coord_x = jnp.tile(jnp.arange(columns, dtype=jnp.float32), row_numbers.shape[0])
        return (coord_x, coord_y)

    def empty_stats(count):
        zeros_line = jnp.zeros((count,), jnp.float32)
        return (jnp.full((count,), -jnp.inf, jnp.float32), zeros_line, zeros_line, zeros_line)

    target_tile = gathered(target_feat, "src").reshape(-1, columns, channels)
    whole_row = jnp.arange(strip_rows * src_count, dtype=jnp.int32)
    tile_x, tile_y = pixel_coords(
        (whole_row // strip_rows * tgt_count + tgt_index) * strip_rows + whole_row % strip_rows
    )
    fixed_flat = target_tile.reshape(-1, channels)
    shard_piece = gathered(source_feat, "tgt").reshape(-1, columns, channels)
    piece_rows = shard_piece.shape[0]
    block_rows = math.gcd(piece_rows, max(1, 512 // columns))
    blocks = piece_rows // block_rows
    block_size = block_rows * columns
    piece_x, piece_y = pixel_coords(
        src_index * tgt_count * strip_rows + jnp.arange(piece_rows, dtype=jnp.int32)
    )

    def block_step(fixed_acc, block_item):
        piece_block, block_x, block_y = block_item
        row_stats, column_stats = tile_stats(
            piece_block, block_x, block_y, fixed_flat, tile_x, tile_y, factor
        )
        return (merge_pair(fixed_acc, column_stats), row_stats)

    fixed_acc, row_parts = lax.scan(
        block_step,
        (empty_stats(target_pixels), empty_stats(source_pixels))[0],
        (
            shard_piece.reshape(blocks, block_size, channels),
            piece_x.reshape(blocks, block_size),
            piece_y.reshape(blocks, block_size),
        ),
    )
    placed = tuple((segment.reshape(-1) for segment in row_parts))
    fixed_acc, piece_acc = (fixed_acc, placed)
    source_stats, target_stats = (piece_acc, fixed_acc)
    own_x, own_y = pixel_coords(
        (src_index * tgt_count + tgt_index) * strip_rows + jnp.arange(strip_rows, dtype=jnp.int32)
    )
    merged_rows = merged(source_stats, "tgt", merge_pair)
    merged_cols = merged(target_stats, "src", merge_pair)
    source_sums = merged_rows[1:]
    target_sums = merged_cols[1:]
    flow_forward = jnp.stack(
        [source_sums[1] / source_sums[0] - own_x, source_sums[2] / source_sums[0] - own_y]
    ).reshape(2, strip_rows, columns)
    flow_backward = jnp.stack(
        [target_sums[1] / target_sums[0] - own_x, target_sums[2] / target_sums[0] - own_y]
    ).reshape(2, strip_rows, columns)
    return (flow_forward, flow_backward)


def on_device(frame_one, frame_two, conv_weight, proj_weight):
    flow_forward, flow_backward, flag = fused(frame_one, frame_two, conv_weight, proj_weight)
    return lax.cond(
        flag[0, 0] > 0.5,
        lambda *_: (flow_forward, flow_backward),
        general,
        frame_one, frame_two, conv_weight, proj_weight,
    )


def solution(mesh):
    in_specs = (P(("src", "tgt"), None, None), P(("src", "tgt"), None, None), P(), P())
    out_specs = (P(None, ("src", "tgt"), None), P(None, ("src", "tgt"), None))
    return jax.shard_map(
        on_device, mesh=mesh, in_specs=in_specs, out_specs=out_specs, check_vma=False
    )
```
